512 devices in a mesh: vocab: 16 (over z_hi, x, core), seq: 32 (over z_lo, y).
Axes of the slice: x: 4, y: 4, z: 16 (z_hi: 2, z_lo: 8; z = z_hi * 8 + z_lo), core: 2. Of those that a mesh axis runs over, the one named last changes fastest.
Arguments:
- token_ids: int32 [2, 2048], P(None, 'seq'), may hold values from 0 to 131071
- keep_mask: int32 [2, 2048], P(None, 'seq'), may hold values 0 or 1
- target_length: int32 [2], replicated, may hold values from 256 to 2048, as said below
- source_length: int32 [2], replicated, may hold values from 128 to 1024, as said below
- embed_table: bfloat16 [131072, 4096], P('vocab', 'seq'), may hold values from -6 to 6
- self_gain: float32 [4096], replicated, may hold values from 0.1 to 1.9
- query_weight: bfloat16 [4096, 2048], P('seq', 'vocab'), may hold values from -0.03125 to 0.03125
- key_weight: bfloat16 [4096, 2048], P('seq', 'vocab'), may hold values from -6 to 6
- value_weight: bfloat16 [4096, 2048], P('seq', 'vocab'), may hold values from -0.09375 to 0.09375
- self_out_weight: bfloat16 [2048, 4096], P('vocab'), may hold values from -0.5 to 0.5
- cross_gain: float32 [4096], replicated, may hold values from 0.1 to 1.9
- cross_query_weight: bfloat16 [4096, 2048], P('seq', 'vocab'), may hold values from -0.03125 to 0.03125
- cross_keys: bfloat16 [2, 1024, 2048], P(None, 'seq', 'vocab'), may hold values from -24 to 24
- cross_values: bfloat16 [2, 1024, 2048], P(None, 'seq', 'vocab'), may hold values from -6 to 6
- cross_out_weight: bfloat16 [2048, 4096], P('vocab'), may hold values from -0.375 to 0.375
Outputs:
- layer_output: bfloat16 [2, 2048, 4096], P(None, 'seq', 'vocab')
The draws below stay inside these ranges and needn't reach their ends.
Inputs may be any that keep to these rules, and one draw needn't show every extreme that they name: `target_length`: the pairs' lengths all differ, and one pair has length 2048. `source_length`: the pairs' lengths all differ, and one pair has length 1024.
All inputs are finite; a program needn't handle non-finite values. No bound on the sum of `keep_mask` on one device may be relied on, other than what follows from the above.
Results may differ from the reference program's by a relative error of at most 0.035.
Values may be sent and summed in bfloat16 or wider, within the bound.
A program may use at most 64 MiB of HBM per device.

```python
import math
import jax
import jax.numpy as jnp
import numpy as np
from jax import lax

D = 4096
DH = 64
HEADS = 32
PAIRS = 2
TOKENS = 2048
SRC = 1024
VOCAB = 131072
HD = 2048
N_VOCAB = 16


def spread_lengths(key, full):
    lowest = full // 8
    picks = jax.random.permutation(key, full - lowest + 1)[:PAIRS].astype(jnp.int32) + lowest
    return jnp.where(picks == jnp.max(picks), full, picks).astype(jnp.int32)


def draw_target_length(key, part):
    return spread_lengths(jax.random.fold_in(key, 5), TOKENS)


def draw_source_length(key, part):
    return spread_lengths(jax.random.fold_in(key, 7), SRC)


def draw_key_weight(key, part):
    key_one = jax.random.fold_in(jax.random.fold_in(key, 11), 0)
    spread = 1.0 / D ** 0.5
    entries = jnp.clip(jax.random.normal(key_one, (D, HEADS * DH), jnp.float32), -6.0, 6.0) * spread
    return jnp.clip(entries, -6.0, 6.0).astype(jnp.bfloat16)


def draw_cross_keys(key, part):
    key_one = jax.random.fold_in(jax.random.fold_in(key, 23), 0)
    entries = jnp.clip(jax.random.normal(key_one, (PAIRS, SRC, HEADS * DH), jnp.float32), -6.0, 6.0)
    return jnp.clip(entries, -24.0, 24.0).astype(jnp.bfloat16)


def plant(values, key, smallest, top_value):
    index_at = [jax.random.randint(jax.random.fold_in(key, axis), (), 0, length) for axis, length in enumerate(values.shape)]
    main_axis = values.shape.index(max(values.shape))
    beside = index_at[:main_axis] + [(index_at[main_axis] + 1) % values.shape[main_axis]] + index_at[main_axis + 1:]
    return values.at[tuple(index_at)].set(smallest).at[tuple(beside)].set(top_value)


def block_levels(key, shape, cuts, least, top_value):
    level = 1.0
    for position, blocks in cuts:
        steps = jax.random.uniform(jax.random.fold_in(jax.random.fold_in(key, 6), position), (blocks,), jnp.float32, least / len(cuts), top_value / len(cuts))
        level = level * jnp.repeat(jnp.exp(steps), shape[position] // blocks).reshape((-1,) + (1,) * (len(shape) - 1 - position))
    return level


def wide_ids(stream_key, shape, number_of, lean):
    loads = [min(1 << octave, number_of + 1 - (1 << octave)) * (1 << 20) // math.isqrt((1 << octave) ** lean) + 1 for octave in range((number_of + 1).bit_length()) if 1 << octave <= number_of]
    width = 1 + sum(loads) // (1 << 30)
    table = np.cumsum(np.array([max(1, weight // width) for weight in loads]))
    pick = jax.random.randint(jax.random.fold_in(stream_key, 1), shape, 0, int(table[len(loads) - 1]))
    start = jnp.left_shift(1, jnp.searchsorted(jnp.asarray(table, jnp.int32), pick, side="right").astype(jnp.int32))
    standing = start - 1 + jax.random.randint(jax.random.fold_in(stream_key, 4), shape, 0, 1 << 30) % jnp.minimum(start, number_of + 1 - start)
    return jax.random.permutation(jax.random.fold_in(stream_key, 2), number_of)[standing].astype(jnp.int32)


def gaussian(rng, dims, scale, most, shards=(), kind=jnp.bfloat16):
    values = jax.random.normal(rng, dims, jnp.float32) * scale
    if len(shards) > 0:
        values = block_levels(rng, dims, shards, -0.22, 0.18) * values
    return jnp.clip(values, min=-most, max=most).astype(kind)


def setup_inputs(seed: int = 0) -> dict:
    key_of = jax.random.split(jax.random.key(seed), 16)
    return {
        "token_ids": plant(wide_ids(key_of[0], (PAIRS, TOKENS), VOCAB, 2), jax.random.fold_in(key_of[0], 3), 0, VOCAB - 1).astype(jnp.int32),
        "keep_mask": plant((jax.random.randint(key_of[1], (PAIRS, TOKENS), 0, 10) < 9).astype(jnp.int32), jax.random.fold_in(key_of[1], 1), 0, 1),
        "target_length": draw_target_length(jax.random.fold_in(key_of[15], 71), 0),
        "source_length": draw_source_length(jax.random.fold_in(key_of[15], 71), 0),
        "embed_table": gaussian(key_of[4], (VOCAB, D), 1.0, 6.0, ((0, 16), (1, 32))),
        "self_gain": jnp.clip(1.0 + 0.18 * jax.random.normal(key_of[5], (D,), jnp.float32), 0.1, 1.9),
        "query_weight": gaussian(key_of[6], (D, HD), (D * DH // 8) ** -0.5, 0.03125, ((0, 32), (1, 16))),
        "key_weight": draw_key_weight(jax.random.fold_in(key_of[15], 71), 0),
        "value_weight": gaussian(key_of[8], (D, HD), D ** -0.5, 0.09375, ((0, 32), (1, 16))),
        "self_out_weight": gaussian(key_of[9], (HD, D), (HD // 16) ** -0.5, 0.5, ((0, 16),)),
        "cross_gain": jnp.clip(1.0 + 0.18 * jax.random.normal(key_of[10], (D,), jnp.float32), 0.1, 1.9),
        "cross_query_weight": gaussian(key_of[11], (D, HD), (D * DH // 8) ** -0.5, 0.03125, ((0, 32), (1, 16))),
        "cross_keys": draw_cross_keys(jax.random.fold_in(key_of[15], 71), 0),
        "cross_values": gaussian(key_of[13], (PAIRS, SRC, HD), 1.0, 6.0, ((1, 32), (2, 16))),
        "cross_out_weight": gaussian(key_of[14], (HD, D), (HD // 8) ** -0.5, 0.375, ((0, 16),)),
    }


def rms_scale(values, gain):
    return values * lax.rsqrt(lax.optimization_barrier(jnp.mean(values * values, axis=-1, keepdims=True)) + 1e-06) * gain

def attend(query, keys, values, visible):
    head_count = query.shape[1] // DH
    q_heads = query.astype(jnp.float32).reshape(query.shape[0], head_count, DH).transpose(1, 0, 2)
    k_heads = keys.astype(jnp.float32).reshape(keys.shape[0], head_count, DH).transpose(1, 0, 2)
    v_heads = values.astype(jnp.float32).reshape(values.shape[0], head_count, DH).transpose(1, 0, 2)

    def single(operands):
        q_one, k_one, v_one = operands
        scores = jnp.dot(q_one, k_one.T, precision=lax.Precision.HIGHEST, preferred_element_type=jnp.float32)
        scores = jnp.where(visible, scores, -jnp.inf)
        raised = jnp.exp(scores - lax.optimization_barrier(jnp.max(scores, axis=-1, keepdims=True)))
        totals = lax.optimization_barrier(jnp.sum(raised, axis=-1, keepdims=True))
        rounded = lax.optimization_barrier(raised.astype(jnp.bfloat16)).astype(jnp.float32)
        mixed = jnp.dot(rounded, v_one, precision=lax.Precision.HIGHEST, preferred_element_type=jnp.float32)
        return mixed / totals
    mixed = lax.map(single, (q_heads, k_heads, v_heads))
    return mixed.transpose(1, 0, 2).reshape(query.shape[0], head_count * DH).astype(jnp.bfloat16)

def group_sum(context, weight):
    group_cols = context.shape[1] // N_VOCAB
    total = jnp.zeros((context.shape[0], weight.shape[1]), jnp.float32)
    for group in range(N_VOCAB):
        lower = group * group_cols
        part_term = jnp.dot(context[:, lower:lower + group_cols], weight[lower:lower + group_cols], preferred_element_type=jnp.float32)
        total = total + lax.optimization_barrier(part_term.astype(jnp.bfloat16)).astype(jnp.float32)
    return total

def one_pair(ids, keep, target_len, source_len, embed_table, self_gain, query_weight, key_weight, value_weight, self_out_weight, cross_gain, cross_query_weight, pair_keys, pair_values, cross_out_weight):
    embedded = embed_table[ids].astype(jnp.float32) * keep.astype(jnp.float32)[:, None]
    self_normed = rms_scale(embedded, self_gain).astype(jnp.bfloat16)
    queries = jnp.dot(self_normed, query_weight, preferred_element_type=jnp.float32).astype(jnp.bfloat16)
    keys = jnp.dot(self_normed, key_weight, preferred_element_type=jnp.float32).astype(jnp.bfloat16)
    values = jnp.dot(self_normed, value_weight, preferred_element_type=jnp.float32).astype(jnp.bfloat16)
    positions = jnp.arange(TOKENS, dtype=jnp.int32)
    visible = (positions[None, :] <= positions[:, None]) & (positions[None, :] < target_len)
    self_context = attend(queries, keys, values, visible)
    after_self = embedded + group_sum(self_context, self_out_weight)
    cross_normed = rms_scale(after_self, cross_gain).astype(jnp.bfloat16)
    cross_queries = jnp.dot(cross_normed, cross_query_weight, preferred_element_type=jnp.float32).astype(jnp.bfloat16)
    source_positions = jnp.arange(SRC, dtype=jnp.int32)
    cross_visible = jnp.broadcast_to((source_positions < source_len)[None, :], (TOKENS, SRC))
    cross_context = attend(cross_queries, pair_keys, pair_values, cross_visible)
    layer_output = after_self + group_sum(cross_context, cross_out_weight)
    return layer_output.astype(jnp.bfloat16)

def reference(token_ids, keep_mask, target_length, source_length, embed_table, self_gain, query_weight, key_weight, value_weight, self_out_weight, cross_gain, cross_query_weight, cross_keys, cross_values, cross_out_weight):
    results = []
    for pair in range(PAIRS):
        results.append(one_pair(token_ids[pair], keep_mask[pair], target_length[pair], source_length[pair], embed_table, self_gain, query_weight, key_weight, value_weight, self_out_weight, cross_gain, cross_query_weight, cross_keys[pair], cross_values[pair], cross_out_weight))
    return jnp.stack(results, axis=0)
```

```python
import functools

import jax
import jax.numpy as jnp
from jax import lax
from jax.experimental import pallas as pl
from jax.experimental.pallas import tpu as pltpu
from jax.sharding import PartitionSpec as P

DH = 64
MESH = pl.DeviceIdType.MESH
F32 = jnp.float32
BF16 = jnp.bfloat16

LINE_Y = ("seq", 4, 1)
LINE_Z = ("seq", 8, 4)
LINE_CORE = ("vocab", 2, 1)
LINE_X = ("vocab", 4, 2)
LINE_ZH = ("vocab", 2, 8)


def place_on(line):
    axis, members, stride = line
    return lax.rem(lax.axis_index(axis) // stride, members)


def peer_of(line, shift):
    axis, members, stride = line
    here = lax.axis_index(axis)
    mine = lax.rem(here // stride, members)
    other = lax.rem(mine + shift, members)
    there = here + (other - mine) * stride
    if axis == "seq":
        return (lax.axis_index("vocab"), there), other
    return (there, lax.axis_index("seq")), other


def push_kernel(line, gather, x_ref, o_ref, own_sem, send_sem, recv_sem):
    members = line[1]
    mine = place_on(line)
    barrier = pltpu.get_barrier_semaphore()
    for shift in range(1, members):
        target, _ = peer_of(line, shift)
        pl.semaphore_signal(barrier, inc=1, device_id=target, device_id_type=MESH)
    own = pltpu.make_async_copy(x_ref if gather else x_ref.at[mine], o_ref.at[mine], own_sem)
    own.start()
    pl.semaphore_wait(barrier, members - 1)
    copies = []
    for shift in range(1, members):
        target, other = peer_of(line, shift)
        copy = pltpu.make_async_remote_copy(
            src_ref=x_ref if gather else x_ref.at[other],
            dst_ref=o_ref.at[mine],
            send_sem=send_sem.at[shift - 1],
            recv_sem=recv_sem.at[shift - 1],
            device_id=target,
            device_id_type=MESH,
        )
        copy.start()
        copies.append(copy)
    own.wait()
    for copy in copies:
        copy.wait()


def push(x, line, ident, gather):
    members = line[1]
    shape = ((members,) + x.shape) if gather else x.shape
    return pl.pallas_call(
        functools.partial(push_kernel, line, gather),
        out_shape=jax.ShapeDtypeStruct(shape, x.dtype),
        in_specs=[pl.BlockSpec(memory_space=pltpu.VMEM)],
        out_specs=pl.BlockSpec(memory_space=pltpu.VMEM),
        scratch_shapes=[
            pltpu.SemaphoreType.DMA,
            pltpu.SemaphoreType.DMA((members - 1,)),
            pltpu.SemaphoreType.DMA((members - 1,)),
        ],
        compiler_params=pltpu.CompilerParams(collective_id=ident, has_side_effects=True),
    )(x)


def relay_kernel(line, x_ref, o_ref, own_sem, up_send, up_recv, down_send, down_recv):
    members = line[1]
    mine = place_on(line)
    barrier = pltpu.get_barrier_semaphore()
    up, _ = peer_of(line, 1)
    down, _ = peer_of(line, members - 1)
    has_up = mine < members - 1
    has_down = mine > 0

    @pl.when(has_up)
    def _():
        pl.semaphore_signal(barrier, inc=1, device_id=up, device_id_type=MESH)

    @pl.when(has_down)
    def _():
        pl.semaphore_signal(barrier, inc=1, device_id=down, device_id_type=MESH)

    own = pltpu.make_async_copy(x_ref, o_ref.at[mine], own_sem)
    own.start()

    @pl.when(has_up & has_down)
    def _():
        pl.semaphore_wait(barrier, 2)

    @pl.when(jnp.logical_not(has_up & has_down))
    def _():
        pl.semaphore_wait(barrier, 1)

    def make(source, target, step, sends, recvs):
        return pltpu.make_async_remote_copy(
            src_ref=x_ref if step == 1 else o_ref.at[source],
            dst_ref=o_ref.at[source],
            send_sem=sends.at[step - 1],
            recv_sem=recvs.at[step - 1],
            device_id=target,
            device_id_type=MESH,
        )

    for step in range(1, members):
        rising = mine - (step - 1)
        falling = mine + (step - 1)

        @pl.when(has_up & (rising >= 0))
        def _():
            make(rising, up, step, up_send, up_recv).start()

        @pl.when(has_down & (falling < members))
        def _():
            make(falling, down, step, down_send, down_recv).start()

        @pl.when(mine - step >= 0)
        def _():
            make(mine - step, up, step, up_send, up_recv).wait_recv()

        @pl.when(mine + step < members)
        def _():
            make(mine + step, down, step, down_send, down_recv).wait_recv()

    for step in range(1, members):

        @pl.when(has_up & (mine - (step - 1) >= 0))
        def _():
            make(mine - (step - 1), up, step, up_send, up_recv).wait_send()

        @pl.when(has_down & (mine + (step - 1) < members))
        def _():
            make(mine + (step - 1), down, step, down_send, down_recv).wait_send()

    own.wait()


def relay(x, line, ident):
    members = line[1]
    sems = pltpu.SemaphoreType.DMA((members - 1,))
    return pl.pallas_call(
        functools.partial(relay_kernel, line),
        out_shape=jax.ShapeDtypeStruct((members,) + x.shape, x.dtype),
        in_specs=[pl.BlockSpec(memory_space=pltpu.VMEM)],
        out_specs=pl.BlockSpec(memory_space=pltpu.VMEM),
        scratch_shapes=[pltpu.SemaphoreType.DMA, sems, sems, sems, sems],
        compiler_params=pltpu.CompilerParams(collective_id=ident, has_side_effects=True),
    )(x)


def fold(blocks):
    return jnp.sum(blocks.astype(F32), axis=0)


def scatter_sum(x, ident):
    x = fold(push(x, LINE_CORE, ident, False)).astype(BF16)
    x = fold(push(x, LINE_X, ident + 1, False)).astype(BF16)
    return fold(push(x, LINE_ZH, ident + 2, False))


def spread(x, ident):
    x = push(x, LINE_ZH, ident, True)
    x = push(x, LINE_X, ident + 1, True)
    return push(x, LINE_CORE, ident + 2, True)


def split_sum(values):
    high = values.astype(BF16)
    low = (values - high.astype(F32)).astype(BF16)
    return high, low


def attend(query, keys, values, visible):
    scores = lax.dot_general(query, keys, (((1,), (1,)), ((), ())), preferred_element_type=F32)
    scores = jnp.where(visible, scores, -jnp.inf)
    raised = jnp.exp(scores - jnp.max(scores, axis=-1, keepdims=True))
    totals = jnp.sum(raised, axis=-1, keepdims=True)
    mixed = jnp.dot(raised.astype(BF16), values, preferred_element_type=F32)
    return (mixed / totals).astype(BF16)


def on_device(
    token_ids,
    keep_mask,
    target_length,
    source_length,
    embed_table,
    self_gain,
    query_weight,
    key_weight,
    value_weight,
    self_out_weight,
    cross_gain,
    cross_query_weight,
    cross_keys,
    cross_values,
    cross_out_weight,
):
    pairs, tokens = token_ids.shape
    vocab_index = lax.axis_index("vocab")
    y_index = place_on(LINE_Y)
    z_index = place_on(LINE_Z)
    n_y, n_z, n_v = LINE_Y[1], LINE_Z[1], lax.axis_size("vocab")
    width = self_gain.shape[0]
    quarter = width // n_y
    cols = embed_table.shape[1]
    heads = 2
    row = n_y * tokens
    row_tokens = pairs * row
    piece = row_tokens // n_v

    ids = jnp.where(keep_mask != 0, token_ids, -1).reshape(1, pairs * tokens)
    ids = push(ids, LINE_Y, 0, True)
    ids = push(ids.reshape(n_y, pairs * tokens), LINE_Z, 1, True)
    ids = ids.reshape(n_z, n_y, pairs, tokens).transpose(0, 2, 1, 3)
    ids = ids.reshape(n_z, n_v, piece).transpose(1, 0, 2).reshape(-1)

    pos = cross_keys.shape[1]
    both = jnp.stack(
        [cross_keys.reshape(pairs, pos, heads, DH), cross_values.reshape(pairs, pos, heads, DH)], axis=3
    )
    both = both.transpose(0, 2, 1, 3, 4).reshape(n_y, pos, 2 * DH)
    both = push(both, LINE_Y, 2, False).reshape(n_y * pos, 2 * DH)
    weights = jnp.concatenate([query_weight, key_weight, value_weight, cross_query_weight, both], axis=1)
    weights = relay(weights, LINE_Z, 3)
    head_cols = query_weight.shape[1]
    weights = weights.reshape(n_z * cols, 4 * head_cols + 2 * DH)
    source_both = weights[:, 4 * head_cols :]

    shard_rows = embed_table.shape[0]
    local_ids = ids - vocab_index * shard_rows
    inside = (local_ids >= 0) & (local_ids < shard_rows)
    picked = jnp.take(embed_table, jnp.clip(local_ids, 0, shard_rows - 1), axis=0)
    picked = jnp.where(inside[:, None], picked, jnp.zeros_like(picked))
    own_rows = scatter_sum(picked.reshape(2, 4, 2, n_z * piece, cols), 4).astype(BF16)
    own_rows = push(own_rows.reshape(n_z, piece, cols), LINE_Z, 7, False)
    own_rows = own_rows.transpose(1, 0, 2).reshape(piece, quarter)
    embedded = spread(own_rows, 8).reshape(row_tokens, quarter)

    def part_of_gain(gain):
        return lax.dynamic_index_in_dim(gain.reshape(n_z, n_y, cols), y_index, 1, False).reshape(quarter)

    wide = embedded.astype(F32)
    squares = jnp.sum(wide * wide, axis=-1)
    scaled = (wide * part_of_gain(self_gain)).astype(BF16)
    partial = jnp.dot(scaled, weights[:, : 3 * head_cols], preferred_element_type=F32).astype(BF16)
    partial = partial.reshape(pairs, row, 3, heads, DH).transpose(0, 3, 1, 2, 4).reshape(n_y, row, 3 * DH)
    high, low = split_sum(squares.reshape(pairs, 1, row))

    def tail(count):
        ends = jnp.stack([high, low], axis=-1)
        ends = jnp.broadcast_to(ends, (pairs, heads, row, 2)).reshape(n_y, row, 2)
        return jnp.pad(ends, ((0, 0), (0, 0), (0, count - 2)))

    summed = fold(push(jnp.concatenate([partial, tail(DH)], axis=2), LINE_Y, 11, False))
    scale = lax.rsqrt((summed[:, 3 * DH] + summed[:, 3 * DH + 1]) / width + 1e-06)
    qkv = (summed[:, : 3 * DH] * scale[:, None]).astype(BF16)
    kv = relay(qkv[:, DH:], LINE_Z, 12).reshape(n_z * row, 2 * DH)

    pair = y_index // heads
    query_pos = z_index * row + lax.broadcasted_iota(jnp.int32, (row, n_z * row), 0)
    key_pos = lax.broadcasted_iota(jnp.int32, (row, n_z * row), 1)
    visible = (key_pos <= query_pos) & (key_pos < lax.dynamic_index_in_dim(target_length, pair, 0, False))
    context = attend(qkv[:, :DH], kv[:, :DH], kv[:, DH:], visible)
    context = push(jnp.pad(context, ((0, 0), (0, DH))), LINE_Y, 13, True)[:, :, :DH]
    context = context.reshape(pairs, heads, row, DH).transpose(0, 2, 1, 3).reshape(row_tokens, heads * DH)
    out_part = lax.dynamic_index_in_dim(self_out_weight.reshape(-1, n_z, n_y, cols), y_index, 2, False)
    terms = jnp.dot(context, out_part.reshape(-1, quarter), preferred_element_type=F32).astype(BF16)
    after = own_rows.astype(F32) + scatter_sum(terms.reshape(2, 4, 2, piece, quarter), 14)
    after = spread(after.astype(BF16), 17).reshape(row_tokens, quarter)

    wide = after.astype(F32)
    squares = jnp.sum(wide * wide, axis=-1)
    scaled = (wide * part_of_gain(cross_gain)).astype(BF16)
    partial = jnp.dot(
        scaled, weights[:, 3 * head_cols : 4 * head_cols], preferred_element_type=F32
    ).astype(BF16)
    partial = partial.reshape(pairs, row, heads, DH).transpose(0, 2, 1, 3).reshape(n_y, row, DH)
    high, low = split_sum(squares.reshape(pairs, 1, row))
    block = lax.dynamic_index_in_dim(after.reshape(row_tokens, n_z, cols), vocab_index // 2, 1, False)
    block = block.reshape(pairs, n_y, tokens, cols).transpose(1, 0, 2, 3).reshape(n_y, pairs * tokens, cols)
    message = jnp.concatenate([jnp.concatenate([partial, tail(DH)], axis=2), block], axis=1)
    message = push(message, LINE_Y, 20, False)
    summed = fold(message[:, :row])
    scale = lax.rsqrt((summed[:, DH] + summed[:, DH + 1]) / width + 1e-06)
    cross_queries = (summed[:, :DH] * scale[:, None]).astype(BF16)
    blocks = message[:, row:].reshape(2, 2, pairs * tokens, cols)
    residual = lax.dynamic_index_in_dim(blocks, lax.rem(vocab_index, 2), 0, False)
    residual = residual.transpose(1, 0, 2).reshape(pairs * tokens, 2 * cols)

    source_pos = lax.broadcasted_iota(jnp.int32, (row, source_both.shape[0]), 1)
    visible = source_pos < lax.dynamic_index_in_dim(source_length, pair, 0, False)
    context = attend(cross_queries, source_both[:, :DH], source_both[:, DH:], visible)
    context = push(jnp.pad(context, ((0, 0), (0, DH))).reshape(n_y, tokens, 2 * DH), LINE_Y, 21, False)
    context = context[:, :, :DH].reshape(pairs, heads, tokens, DH).transpose(0, 2, 1, 3)
    context = context.reshape(pairs * tokens, heads * DH)
    terms = jnp.dot(context, cross_out_weight, preferred_element_type=F32).astype(BF16)
    share = width // n_v
    terms = terms.reshape(pairs * tokens, 2, 4, 2, share).transpose(3, 2, 1, 0, 4)
    result = residual.astype(F32) + scatter_sum(terms, 22)
    return result.astype(BF16).reshape(pairs, tokens, share)


def solution(mesh):
    return jax.shard_map(
        on_device,
        mesh=mesh,
        in_specs=(
            P(None, "seq"),
            P(None, "seq"),
            P(),
            P(),
            P("vocab", "seq"),
            P(),
            P("seq", "vocab"),
            P("seq", "vocab"),
            P("seq", "vocab"),
            P("vocab", None),
            P(),
            P("seq", "vocab"),
            P(None, "seq", "vocab"),
            P(None, "seq", "vocab"),
            P("vocab", None),
        ),
        out_specs=P(None, "seq", "vocab"),
        check_vma=False,
    )
```

```python
import functools

import jax
import jax.numpy as jnp
from jax import lax
from jax.experimental import pallas as pl
from jax.experimental.pallas import tpu as pltpu
from jax.sharding import PartitionSpec as P

DH = 64
MESH = pl.DeviceIdType.MESH
F32 = jnp.float32
BF16 = jnp.bfloat16

LINE_Y = ("seq", 4, 1)
LINE_Z = ("seq", 8, 4)
LINE_CORE = ("vocab", 2, 1)
LINE_X = ("vocab", 4, 2)
LINE_ZH = ("vocab", 2, 8)


def place_on(line):
    axis, members, stride = line
    return lax.rem(lax.axis_index(axis) // stride, members)


def peer_of(line, shift):
    axis, members, stride = line
    here = lax.axis_index(axis)
    mine = lax.rem(here // stride, members)
    other = lax.rem(mine + shift, members)
    there = here + (other - mine) * stride
    if axis == "seq":
        return (lax.axis_index("vocab"), there), other
    return (there, lax.axis_index("seq")), other


def push_kernel(line, gather, x_ref, o_ref, own_sem, send_sem, recv_sem):
    members = line[1]
    mine = place_on(line)
    barrier = pltpu.get_barrier_semaphore()
    for shift in range(1, members):
        target, _ = peer_of(line, shift)
        pl.semaphore_signal(barrier, inc=1, device_id=target, device_id_type=MESH)
    own = pltpu.make_async_copy(x_ref if gather else x_ref.at[mine], o_ref.at[mine], own_sem)
    own.start()
    pl.semaphore_wait(barrier, members - 1)
    copies = []
    for shift in range(1, members):
        target, other = peer_of(line, shift)
        copy = pltpu.make_async_remote_copy(
            src_ref=x_ref if gather else x_ref.at[other],
            dst_ref=o_ref.at[mine],
            send_sem=send_sem.at[shift - 1],
            recv_sem=recv_sem.at[shift - 1],
            device_id=target,
            device_id_type=MESH,
        )
        copy.start()
        copies.append(copy)
    own.wait()
    for copy in copies:
        copy.wait()


def push(x, line, ident, gather):
    members = line[1]
    shape = ((members,) + x.shape) if gather else x.shape
    return pl.pallas_call(
        functools.partial(push_kernel, line, gather),
        out_shape=jax.ShapeDtypeStruct(shape, x.dtype),
        in_specs=[pl.BlockSpec(memory_space=pltpu.VMEM)],
        out_specs=pl.BlockSpec(memory_space=pltpu.VMEM),
        scratch_shapes=[
            pltpu.SemaphoreType.DMA,
            pltpu.SemaphoreType.DMA((members - 1,)),
            pltpu.SemaphoreType.DMA((members - 1,)),
        ],
        compiler_params=pltpu.CompilerParams(collective_id=ident, has_side_effects=True),
    )(x)


def relay_kernel(line, x_ref, o_ref, own_sem, up_send, up_recv, down_send, down_recv):
    members = line[1]
    mine = place_on(line)
    barrier = pltpu.get_barrier_semaphore()
    up, _ = peer_of(line, 1)
    down, _ = peer_of(line, members - 1)
    has_up = mine < members - 1
    has_down = mine > 0

    @pl.when(has_up)
    def _():
        pl.semaphore_signal(barrier, inc=1, device_id=up, device_id_type=MESH)

    @pl.when(has_down)
    def _():
        pl.semaphore_signal(barrier, inc=1, device_id=down, device_id_type=MESH)

    own = pltpu.make_async_copy(x_ref, o_ref.at[mine], own_sem)
    own.start()

    @pl.when(has_up & has_down)
    def _():
        pl.semaphore_wait(barrier, 2)

    @pl.when(jnp.logical_not(has_up & has_down))
    def _():
        pl.semaphore_wait(barrier, 1)

    def make(source, target, step, sends, recvs):
        return pltpu.make_async_remote_copy(
            src_ref=x_ref if step == 1 else o_ref.at[source],
            dst_ref=o_ref.at[source],
            send_sem=sends.at[step - 1],
            recv_sem=recvs.at[step - 1],
            device_id=target,
            device_id_type=MESH,
        )

    for step in range(1, members):
        rising = mine - (step - 1)
        falling = mine + (step - 1)

        @pl.when(has_up & (rising >= 0))
        def _():
            make(rising, up, step, up_send, up_recv).start()

        @pl.when(has_down & (falling < members))
        def _():
            make(falling, down, step, down_send, down_recv).start()

        @pl.when(mine - step >= 0)
        def _():
            make(mine - step, up, step, up_send, up_recv).wait_recv()

        @pl.when(mine + step < members)
        def _():
            make(mine + step, down, step, down_send, down_recv).wait_recv()

    for step in range(1, members):

        @pl.when(has_up & (mine - (step - 1) >= 0))
        def _():
            make(mine - (step - 1), up, step, up_send, up_recv).wait_send()

        @pl.when(has_down & (mine + (step - 1) < members))
        def _():
            make(mine + (step - 1), down, step, down_send, down_recv).wait_send()

    own.wait()


def relay(x, line, ident):
    members = line[1]
    sems = pltpu.SemaphoreType.DMA((members - 1,))
    return pl.pallas_call(
        functools.partial(relay_kernel, line),
        out_shape=jax.ShapeDtypeStruct((members,) + x.shape, x.dtype),
        in_specs=[pl.BlockSpec(memory_space=pltpu.VMEM)],
        out_specs=pl.BlockSpec(memory_space=pltpu.VMEM),
        scratch_shapes=[pltpu.SemaphoreType.DMA, sems, sems, sems, sems],
        compiler_params=pltpu.CompilerParams(collective_id=ident, has_side_effects=True),
    )(x)


def fold(blocks):
    return jnp.sum(blocks.astype(F32), axis=0)


def vocab_kernel(mode, *refs):
    if mode == "rows":
        x_ref, own_ref, all_ref = refs[:3]
        refs = refs[3:]
    elif mode == "terms":
        x_ref, base_ref, all_ref = refs[:3]
        refs = refs[3:]
    else:
        x_ref, own_ref = refs[:2]
        refs = refs[2:]
    got_core, part, got_x, half, got_zh, piece = refs[:6]
    core_s, core_r, x_s, x_r, zh_s, zh_r, z_s, z_r, x2_s, x2_r, core2_s, core2_r, local = refs[6:]
    core, place, z, zh = place_on(LINE_CORE), place_on(LINE_X), place_on(LINE_Z), place_on(LINE_ZH)
    lines = [LINE_CORE, LINE_X, LINE_ZH] + ([LINE_Z] if mode == "rows" else [])
    barrier = pltpu.get_barrier_semaphore()
    met = 0
    for line in lines:
        for shift in range(1, line[1]):
            target, _ = peer_of(line, shift)
            pl.semaphore_signal(barrier, inc=1, device_id=target, device_id_type=MESH)
            met += 1
    pl.semaphore_wait(barrier, met)

    def send(source, target_ref, line, shift, send_sem, recv_sem):
        copy = pltpu.make_async_remote_copy(
            src_ref=source,
            dst_ref=target_ref,
            send_sem=send_sem,
            recv_sem=recv_sem,
            device_id=peer_of(line, shift)[0],
            device_id_type=MESH,
        )
        copy.start()
        return copy

    core_copies = []
    for shift in (1, 2, 3, 0):
        other = lax.rem(place + shift, 4)
        core_copies.append(
            send(x_ref.at[1 - core, other], got_core.at[other], LINE_CORE, 1, core_s.at[shift], core_r.at[shift])
        )
    x_copies = []
    for order, shift in enumerate((1, 2, 3, 0)):
        other = lax.rem(place + shift, 4)
        core_copies[order].wait()
        part[other] = (x_ref[core, other].astype(F32) + got_core[other].astype(F32)).astype(BF16)
        if shift:
            x_copies.append(
                send(part.at[other], got_x.at[shift - 1], LINE_X, shift, x_s.at[shift - 1], x_r.at[shift - 1])
            )
    total = part[place].astype(F32)
    for shift in range(1, 4):
        x_copies[shift - 1].wait()
        total = total + got_x[shift - 1].astype(F32)
    half[...] = total.astype(BF16)
    if mode == "final":
        send(half.at[1 - zh], got_zh, LINE_ZH, 1, zh_s, zh_r).wait()
        own_ref[...] = half[zh].astype(F32) + got_zh[...].astype(F32)
        return
    send(half, got_zh, LINE_ZH, 1, zh_s, zh_r).wait()
    total = half[...].astype(F32) + got_zh[...].astype(F32)
    if mode == "rows":
        piece[...] = total.astype(BF16)
        cols = piece.shape[2]
        mine = pl.ds(pl.multiple_of(z * cols, cols), cols)
        z_copies = []
        for shift in range(1, LINE_Z[1]):
            _, other = peer_of(LINE_Z, shift)
            z_copies.append(
                send(piece.at[other], own_ref.at[:, mine], LINE_Z, shift, z_s.at[shift - 1], z_r.at[shift - 1])
            )
        own_ref[:, mine] = piece[z]
        for copy in z_copies:
            copy.wait()
        block = own_ref
    else:
        piece[...] = (base_ref[...].astype(F32) + total).astype(BF16)
        block = piece
    keep = pltpu.make_async_copy(block, all_ref.at[core, place], local)
    keep.start()
    copies = [send(block, all_ref.at[core, place], LINE_CORE, 1, core2_s.at[0], core2_r.at[0])]
    x_copies = []
    for shift in range(1, 4):
        x_copies.append(
            send(block, all_ref.at[core, place], LINE_X, shift, x2_s.at[shift - 1], x2_r.at[shift - 1])
        )
    for shift in range(1, 4):
        x_copies[shift - 1].wait()
        source = lax.rem(place + 4 - shift, 4)
        copies.append(
            send(all_ref.at[core, source], all_ref.at[core, source], LINE_CORE, 1, core2_s.at[shift], core2_r.at[shift])
        )
    for copy in copies:
        copy.wait()
    keep.wait()


def vocab_call(mode, ident, x, base=None):
    block = x.shape[2:]
    vmem = pl.BlockSpec(memory_space=pltpu.VMEM)
    if mode == "rows":
        own = (block[1], block[0] * block[2])
        out = (jax.ShapeDtypeStruct(own, BF16), jax.ShapeDtypeStruct((2, 4) + own, BF16))
    elif mode == "terms":
        out = jax.ShapeDtypeStruct(x.shape, BF16)
    else:
        out = jax.ShapeDtypeStruct(block[1:], F32)
    operands = (x,) if base is None else (x, base)
    crossing = block[1:] if mode == "final" else block

    def sems(count):
        return [pltpu.SemaphoreType.DMA((count,))] * 2

    single = pltpu.SemaphoreType.DMA
    return pl.pallas_call(
        functools.partial(vocab_kernel, mode),
        out_shape=out,
        in_specs=[vmem] * len(operands),
        out_specs=(vmem, vmem) if mode == "rows" else vmem,
        scratch_shapes=[
            pltpu.VMEM((4,) + block, BF16),
            pltpu.VMEM((4,) + block, BF16),
            pltpu.VMEM((3,) + block, BF16),
            pltpu.VMEM(block, BF16),
            pltpu.VMEM(crossing, BF16),
            pltpu.VMEM(block, BF16),
        ]
        + sems(4) + sems(3) + [single, single] + sems(7) + sems(3) + sems(4) + [single],
        compiler_params=pltpu.CompilerParams(collective_id=ident, has_side_effects=True),
    )(*operands)


def split_sum(values):
    high = values.astype(BF16)
    low = (values - high.astype(F32)).astype(BF16)
    return high, low


def attend(query, keys, values, visible):
    scores = lax.dot_general(query, keys, (((1,), (1,)), ((), ())), preferred_element_type=F32)
    scores = jnp.where(visible, scores, -jnp.inf)
    raised = jnp.exp(scores - jnp.max(scores, axis=-1, keepdims=True))
    totals = jnp.sum(raised, axis=-1, keepdims=True)
    mixed = jnp.dot(raised.astype(BF16), values, preferred_element_type=F32)
    return (mixed / totals).astype(BF16)


def on_device(
    token_ids,
    keep_mask,
    target_length,
    source_length,
    embed_table,
    self_gain,
    query_weight,
    key_weight,
    value_weight,
    self_out_weight,
    cross_gain,
    cross_query_weight,
    cross_keys,
    cross_values,
    cross_out_weight,
):
    pairs, tokens = token_ids.shape
    vocab_index = lax.axis_index("vocab")
    y_index = place_on(LINE_Y)
    z_index = place_on(LINE_Z)
    n_y, n_z, n_v = LINE_Y[1], LINE_Z[1], lax.axis_size("vocab")
    width = self_gain.shape[0]
    quarter = width // n_y
    cols = embed_table.shape[1]
    heads = 2
    row = n_y * tokens
    row_tokens = pairs * row
    pieces = n_v // LINE_ZH[1]
    piece = row_tokens // pieces

    ids = jnp.where(keep_mask != 0, token_ids, -1).reshape(1, pairs * tokens)
    ids = push(ids, LINE_Y, 0, True)
    ids = push(ids.reshape(n_y, pairs * tokens), LINE_Z, 1, True)
    ids = ids.reshape(n_z, n_y, pairs, tokens).transpose(0, 2, 1, 3)
    ids = ids.reshape(n_z, pieces, piece).transpose(1, 0, 2).reshape(-1)

    pos = cross_keys.shape[1]
    both = jnp.stack(
        [cross_keys.reshape(pairs, pos, heads, DH), cross_values.reshape(pairs, pos, heads, DH)], axis=3
    )
    both = both.transpose(0, 2, 1, 3, 4).reshape(n_y, pos, 2 * DH)
    both = push(both, LINE_Y, 2, False).reshape(n_y * pos, 2 * DH)
    weights = jnp.concatenate([query_weight, key_weight, value_weight, cross_query_weight, both], axis=1)
    same_y = [[z * n_y + y for z in range(n_z)] for y in range(n_y)]
    weights = lax.all_gather(weights, "seq", axis_index_groups=same_y)
    head_cols = query_weight.shape[1]
    weights = weights.reshape(n_z * cols, 4 * head_cols + 2 * DH)
    source_both = weights[:, 4 * head_cols :]

    shard_rows = embed_table.shape[0]
    local_ids = ids - vocab_index * shard_rows
    inside = (local_ids >= 0) & (local_ids < shard_rows)
    picked = jnp.take(embed_table, jnp.clip(local_ids, 0, shard_rows - 1), axis=0)
    picked = jnp.where(inside[:, None], picked, jnp.zeros_like(picked))
    own_rows, embedded = vocab_call("rows", 4, picked.reshape(2, 4, n_z, piece, cols))
    embedded = embedded.reshape(row_tokens, quarter)

    def part_of_gain(gain):
        return lax.dynamic_index_in_dim(gain.reshape(n_z, n_y, cols), y_index, 1, False).reshape(quarter)

    wide = embedded.astype(F32)
    squares = jnp.sum(wide * wide, axis=-1)
    scaled = (wide * part_of_gain(self_gain)).astype(BF16)
    partial = jnp.dot(scaled, weights[:, : 3 * head_cols], preferred_element_type=F32).astype(BF16)
    partial = partial.reshape(pairs, row, 3, heads, DH).transpose(0, 3, 1, 2, 4).reshape(n_y, row, 3 * DH)
    high, low = split_sum(squares.reshape(pairs, 1, row))

    def tail(count):
        ends = jnp.stack([high, low], axis=-1)
        ends = jnp.broadcast_to(ends, (pairs, heads, row, 2)).reshape(n_y, row, 2)
        return jnp.pad(ends, ((0, 0), (0, 0), (0, count - 2)))

    summed = fold(push(jnp.concatenate([partial, tail(DH)], axis=2), LINE_Y, 11, False))
    scale = lax.rsqrt((summed[:, 3 * DH] + summed[:, 3 * DH + 1]) / width + 1e-06)
    qkv = (summed[:, : 3 * DH] * scale[:, None]).astype(BF16)
    kv = relay(qkv[:, DH:], LINE_Z, 12).reshape(n_z * row, 2 * DH)

    pair = y_index // heads
    query_pos = z_index * row + lax.broadcasted_iota(jnp.int32, (row, n_z * row), 0)
    key_pos = lax.broadcasted_iota(jnp.int32, (row, n_z * row), 1)
    visible = (key_pos <= query_pos) & (key_pos < lax.dynamic_index_in_dim(target_length, pair, 0, False))
    context = attend(qkv[:, :DH], kv[:, :DH], kv[:, DH:], visible)
    context = push(jnp.pad(context, ((0, 0), (0, DH))), LINE_Y, 13, True)[:, :, :DH]
    context = context.reshape(pairs, heads, row, DH).transpose(0, 2, 1, 3).reshape(row_tokens, heads * DH)
    out_part = lax.dynamic_index_in_dim(self_out_weight.reshape(-1, n_z, n_y, cols), y_index, 2, False)
    terms = jnp.dot(context, out_part.reshape(-1, quarter), preferred_element_type=F32).astype(BF16)
    after = vocab_call("terms", 5, terms.reshape(2, 4, piece, quarter), own_rows)
    after = after.reshape(row_tokens, quarter)

    wide = after.astype(F32)
    squares = jnp.sum(wide * wide, axis=-1)
    scaled = (wide * part_of_gain(cross_gain)).astype(BF16)
    partial = jnp.dot(
        scaled, weights[:, 3 * head_cols : 4 * head_cols], preferred_element_type=F32
    ).astype(BF16)
    partial = partial.reshape(pairs, row, heads, DH).transpose(0, 2, 1, 3).reshape(n_y, row, DH)
    high, low = split_sum(squares.reshape(pairs, 1, row))
    block = lax.dynamic_index_in_dim(after.reshape(row_tokens, n_z, cols), vocab_index // 2, 1, False)
    block = block.reshape(pairs, n_y, tokens, cols).transpose(1, 0, 2, 3).reshape(n_y, pairs * tokens, cols)
    message = jnp.concatenate([jnp.concatenate([partial, tail(DH)], axis=2), block], axis=1)
    message = push(message, LINE_Y, 20, False)
    summed = fold(message[:, :row])
    scale = lax.rsqrt((summed[:, DH] + summed[:, DH + 1]) / width + 1e-06)
    cross_queries = (summed[:, :DH] * scale[:, None]).astype(BF16)
    blocks = message[:, row:].reshape(2, 2, pairs * tokens, cols)
    residual = lax.dynamic_index_in_dim(blocks, lax.rem(vocab_index, 2), 0, False)
    residual = residual.transpose(1, 0, 2).reshape(pairs * tokens, 2 * cols)

    source_pos = lax.broadcasted_iota(jnp.int32, (row, source_both.shape[0]), 1)
    visible = source_pos < lax.dynamic_index_in_dim(source_length, pair, 0, False)
    context = attend(cross_queries, source_both[:, :DH], source_both[:, DH:], visible)
    context = push(jnp.pad(context, ((0, 0), (0, DH))).reshape(n_y, tokens, 2 * DH), LINE_Y, 21, False)
    context = context[:, :, :DH].reshape(pairs, heads, tokens, DH).transpose(0, 2, 1, 3)
    context = context.reshape(pairs * tokens, heads * DH)
    terms = jnp.dot(context, cross_out_weight, preferred_element_type=F32).astype(BF16)
    share = width // n_v
    terms = terms.reshape(pairs * tokens, 2, 4, 2, share).transpose(3, 2, 1, 0, 4)
    result = residual.astype(F32) + vocab_call("final", 6, terms)
    return result.astype(BF16).reshape(pairs, tokens, share)


def solution(mesh):
    return jax.shard_map(
        on_device,
        mesh=mesh,
        in_specs=(
            P(None, "seq"),
            P(None, "seq"),
            P(),
            P(),
            P("vocab", "seq"),
            P(),
            P("seq", "vocab"),
            P("seq", "vocab"),
            P("seq", "vocab"),
            P("vocab", None),
            P(),
            P("seq", "vocab"),
            P(None, "seq", "vocab"),
            P(None, "seq", "vocab"),
            P("vocab", None),
        ),
        out_specs=P(None, "seq", "vocab"),
        check_vma=False,
    )
```

```python
import functools

import jax
import jax.numpy as jnp
from jax import lax
from jax.experimental import pallas as pl
from jax.experimental.pallas import tpu as pltpu
from jax.sharding import PartitionSpec as P

DH = 64
MESH = pl.DeviceIdType.MESH
F32 = jnp.float32
BF16 = jnp.bfloat16

LINE_Y = ("seq", 4, 1)
LINE_Z = ("seq", 8, 4)
LINE_CORE = ("vocab", 2, 1)
LINE_X = ("vocab", 4, 2)
LINE_ZH = ("vocab", 2, 8)


def place_on(line):
    axis, members, stride = line
    return lax.rem(lax.axis_index(axis) // stride, members)


def peer_of(line, shift):
    axis, members, stride = line
    here = lax.axis_index(axis)
    mine = lax.rem(here // stride, members)
    other = lax.rem(mine + shift, members)
    there = here + (other - mine) * stride
    if axis == "seq":
        return (lax.axis_index("vocab"), there), other
    return (there, lax.axis_index("seq")), other


def greet(devices):
    barrier = pltpu.get_barrier_semaphore()
    for target in devices:
        pl.semaphore_signal(barrier, inc=1, device_id=target, device_id_type=MESH)
    return barrier


def peers_on(line):
    return [peer_of(line, shift)[0] for shift in range(1, line[1])]


def send(source, target_ref, target, send_sem, recv_sem):
    copy = pltpu.make_async_remote_copy(
        src_ref=source,
        dst_ref=target_ref,
        send_sem=send_sem,
        recv_sem=recv_sem,
        device_id=target,
        device_id_type=MESH,
    )
    copy.start()
    return copy


def start_kernel(ids_ref, both_ref, all_ids, both_out, row_ids, own, y_s, y_r, z_s, z_r, b_s, b_r):
    y, z = place_on(LINE_Y), place_on(LINE_Z)
    near, far = peers_on(LINE_Y), peers_on(LINE_Z)
    barrier = greet(near + far)
    keep = [
        pltpu.make_async_copy(ids_ref, row_ids.at[y], own.at[0]),
        pltpu.make_async_copy(both_ref.at[y], both_out.at[y], own.at[1]),
    ]
    for copy in keep:
        copy.start()
    pl.semaphore_wait(barrier, len(near + far))
    copies = [send(ids_ref, row_ids.at[y], near[k], y_s.at[k], y_r.at[k]) for k in range(3)]
    later = []
    for k in range(3):
        other = lax.rem(y + k + 1, 4)
        later.append(send(both_ref.at[other], both_out.at[y], near[k], b_s.at[k], b_r.at[k]))
    for copy in keep + copies:
        copy.wait()
    last = pltpu.make_async_copy(row_ids, all_ids.at[z], own.at[2])
    last.start()
    later += [send(row_ids, all_ids.at[z], far[k], z_s.at[k], z_r.at[k]) for k in range(7)]
    for copy in later + [last]:
        copy.wait()


def sems(count):
    return [pltpu.SemaphoreType.DMA((count,))] * 2


def call(kernel, ident, out, scratch, operands, in_specs=None):
    vmem = pl.BlockSpec(memory_space=pltpu.VMEM)
    return pl.pallas_call(
        kernel,
        out_shape=out,
        in_specs=in_specs or [vmem] * len(operands),
        out_specs=(vmem,) * len(out) if isinstance(out, tuple) else vmem,
        scratch_shapes=scratch,
        compiler_params=pltpu.CompilerParams(collective_id=ident, has_side_effects=True),
    )(*operands)


def near_sum(x_ref, got_core, part, got_x, half, core_s, core_r, x_s, x_r):
    core, place = place_on(LINE_CORE), place_on(LINE_X)
    twin, row = peers_on(LINE_CORE)[0], peers_on(LINE_X)
    order = (1, 2, 3, 0)
    core_copies = []
    for k, shift in enumerate(order):
        other = lax.rem(place + shift, 4)
        core_copies.append(send(x_ref.at[1 - core, other], got_core.at[other], twin, core_s.at[k], core_r.at[k]))
    x_copies = []
    for k, shift in enumerate(order):
        other = lax.rem(place + shift, 4)
        core_copies[k].wait()
        part[other] = (x_ref[core, other].astype(F32) + got_core[other].astype(F32)).astype(BF16)
        if shift:
            x_copies.append(send(part.at[other], got_x.at[k], row[k], x_s.at[k], x_r.at[k]))
    total = part[place].astype(F32)
    for k in range(3):
        x_copies[k].wait()
        total = total + got_x[k].astype(F32)
    half[...] = total.astype(BF16)


def near_sum_scratch(block):
    return [
        pltpu.VMEM((4,) + block, BF16),
        pltpu.VMEM((4,) + block, BF16),
        pltpu.VMEM((3,) + block, BF16),
        pltpu.VMEM(block, BF16),
    ] + sems(4) + sems(3)


def spread(block, all_ref, core_s, core_r, x_s, x_r, local):
    core, place = place_on(LINE_CORE), place_on(LINE_X)
    twin, row = peers_on(LINE_CORE)[0], peers_on(LINE_X)
    keep = pltpu.make_async_copy(block, all_ref.at[core, place], local)
    keep.start()
    copies = [send(block, all_ref.at[core, place], twin, core_s.at[0], core_r.at[0])]
    x_copies = [send(block, all_ref.at[core, place], row[k], x_s.at[k], x_r.at[k]) for k in range(3)]
    for k in range(3):
        x_copies[k].wait()
        source = all_ref.at[core, lax.rem(place + 3 - k, 4)]
        copies.append(send(source, source, twin, core_s.at[k + 1], core_r.at[k + 1]))
    for copy in copies:
        copy.wait()
    keep.wait()


def spread_scratch():
    return sems(4) + sems(3) + [pltpu.SemaphoreType.DMA]


def rows_kernel(x_ref, own_ref, all_ref, *refs):
    near, refs = refs[:8], refs[8:]
    got, z_s, z_r, zh_s, zh_r = refs[:5]
    half = near[3]
    z, zh = place_on(LINE_Z), place_on(LINE_ZH)
    v, s = lax.axis_index("vocab"), lax.axis_index("seq")
    level = peers_on(LINE_Z)
    over_v = peer_of(LINE_ZH, 1)[0][0]
    across = [(over_v, peer_of(LINE_Z, k)[0][1]) for k in range(8)]
    devices = peers_on(LINE_CORE) + peers_on(LINE_X) + level + across
    barrier = greet(devices)
    pl.semaphore_wait(barrier, len(devices))
    near_sum(x_ref, *near)
    copies = []
    for k in (4, 3, 5, 2, 6, 1, 7, 0):
        other = lax.rem(z + k, 8)
        copies.append(send(half.at[other], got.at[zh, z], across[k], zh_s.at[k], zh_r.at[k]))
        if k:
            copies.append(send(half.at[other], got.at[zh, z], level[k - 1], z_s.at[k - 1], z_r.at[k - 1]))
    got[zh, z] = half[z]
    for copy in copies:
        copy.wait()
    cols = got.shape[3]
    for k in range(8):
        own_ref[:, k * cols : (k + 1) * cols] = (got[0, k].astype(F32) + got[1, k].astype(F32)).astype(BF16)
    spread(own_ref, all_ref, *refs[5:])


def embed_rows(x, ident):
    block = x.shape[2:]
    own = (block[1], block[0] * block[2])
    out = (jax.ShapeDtypeStruct(own, BF16), jax.ShapeDtypeStruct((2, 4) + own, BF16))
    scratch = near_sum_scratch(block) + [pltpu.VMEM((2,) + block, BF16)] + sems(7) + sems(8) + spread_scratch()
    return call(rows_kernel, ident, out, scratch, (x,))


def lanes_of(shape):
    return lax.broadcasted_iota(jnp.int32, shape, 1)


def with_squares(product, squares, lane):
    high = squares.astype(BF16).astype(F32)
    at = lanes_of(product.shape)
    return jnp.where(at == lane, high, jnp.where(at == lane + 1, squares - high, product))


def scaled_sum(got, rows, lane, width):
    total = got[0, :rows].astype(F32)
    for k in range(1, 4):
        total = total + got[k, :rows].astype(F32)
    squares = total[:, lane : lane + 1] + total[:, lane + 1 : lane + 2]
    return total * lax.rsqrt(squares / width + 1e-06)


def attend(query, both, visible, head):
    scores = lax.dot_general(query, both, (((1,), (1,)), ((), ())), preferred_element_type=F32)
    scores = jnp.where(visible, scores, -jnp.inf)
    raised = jnp.exp(scores - jnp.max(scores, axis=-1, keepdims=True))
    totals = jnp.sum(raised, axis=-1, keepdims=True)
    mixed = jnp.dot(raised.astype(BF16), both, preferred_element_type=F32) / totals
    moved = jnp.where(head == 0, pltpu.roll(mixed, DH, 1), mixed)
    return jnp.where(lanes_of(moved.shape) // DH == head, moved, 0.0).astype(BF16)


def self_kernel(width, length_ref, emb_ref, own_ref, gain_ref, weight_ref, out_ref, all_ref, *refs):
    blocks, got_y, kv, got_ctx, terms, y_s, y_r, up_s, up_r, c_s, c_r, got_zh, piece, zh_s, zh_r = refs[:15]
    near, far = refs[15:23], refs[23:]
    half = near[3]
    y, z = place_on(LINE_Y), place_on(LINE_Z)
    side = peers_on(LINE_Y)
    up, down = peer_of(LINE_Z, 1)[0], peer_of(LINE_Z, 7)[0]
    has_up, has_down = z < 7, z > 0
    devices = peers_on(LINE_CORE) + peers_on(LINE_X) + peers_on(LINE_ZH) + side
    barrier = greet(devices)

    @pl.when(has_up)
    def _():
        pl.semaphore_signal(barrier, inc=1, device_id=up, device_id_type=MESH)

    @pl.when(has_down)
    def _():
        pl.semaphore_signal(barrier, inc=1, device_id=down, device_id_type=MESH)

    row = emb_ref.shape[0] // 2
    for pair in range(2):
        wide = emb_ref[pair * row : (pair + 1) * row].astype(F32)
        squares = jnp.sum(wide * wide, axis=-1, keepdims=True)
        scaled = (wide * gain_ref[...]).astype(BF16)
        for head in range(2):
            weight = weight_ref[:, head * 4 * DH : (head + 1) * 4 * DH]
            product = jnp.dot(scaled, weight, preferred_element_type=F32)
            blocks[2 * pair + head] = with_squares(product, squares, 3 * DH).astype(BF16)
    for k in range(1, 8):

        @pl.when(k > z)
        def _():
            kv[k] = jnp.zeros(kv.shape[1:], BF16)

    @pl.when(has_up & has_down)
    def _():
        pl.semaphore_wait(barrier, len(devices) + 2)

    @pl.when(jnp.logical_not(has_up & has_down))
    def _():
        pl.semaphore_wait(barrier, len(devices) + 1)

    copies = []
    for k in range(3):
        other = lax.rem(y + k + 1, 4)
        copies.append(send(blocks.at[other], got_y.at[y], side[k], y_s.at[k], y_r.at[k]))
    got_y[y] = blocks[y]
    for copy in copies:
        copy.wait()
    qkv = scaled_sum(got_y, row, 3 * DH, width)
    kv[z] = qkv[:, : 2 * DH].astype(BF16)
    query = qkv[:, 2 * DH :]
    query = jnp.where(lanes_of(query.shape) < DH, query, 0.0).astype(BF16)

    chunk = row // 2

    def passing(source, step, part):
        place = kv.at[source, part * chunk : (part + 1) * chunk]
        index = (step - 1) * 2 + part
        return pltpu.make_async_remote_copy(
            src_ref=place,
            dst_ref=place,
            send_sem=up_s.at[index],
            recv_sem=up_r.at[index],
            device_id=up,
            device_id_type=MESH,
        )

    for step in range(1, 9):
        for part in range(2):
            if step > 1:

                @pl.when(z - step + 1 >= 0)
                def _():
                    passing(z - step + 1, step - 1, part).wait_recv()

            if step < 8:

                @pl.when(has_up & (z - step + 1 >= 0))
                def _():
                    passing(z - step + 1, step, part).start()

    pair = y // 2
    both = kv[...].reshape(8 * row, 2 * DH)
    key_pos = lanes_of((row, 8 * row))
    query_pos = z * row + lax.broadcasted_iota(jnp.int32, (row, 8 * row), 0)
    visible = (key_pos <= query_pos) & (key_pos < length_ref[pair])
    got_ctx[y] = attend(query, both, visible, lax.rem(y, 2))
    copies = [send(got_ctx.at[y], got_ctx.at[y], side[k], c_s.at[k], c_r.at[k]) for k in range(3)]
    for step in range(1, 8):
        for part in range(2):

            @pl.when(has_up & (z - step + 1 >= 0))
            def _():
                passing(z - step + 1, step, part).wait_send()

    for copy in copies:
        copy.wait()
    for pair in range(2):
        context = got_ctx[2 * pair] + got_ctx[2 * pair + 1]
        product = jnp.dot(context, out_ref[...], preferred_element_type=F32).astype(BF16)
        terms[pair] = product.reshape(terms.shape[1:])
    near_sum(terms, *near)
    send(half, got_zh, peers_on(LINE_ZH)[0], zh_s.at[0], zh_r.at[0]).wait()
    piece[...] = (own_ref[...].astype(F32) + (half[...].astype(F32) + got_zh[...].astype(F32))).astype(BF16)
    spread(piece, all_ref, *far)


def self_block(ident, width, length, embedded, own_rows, gain, weights, out_weight):
    tokens, quarter = embedded.shape
    row = tokens // 2
    piece = own_rows.shape
    vmem = pl.BlockSpec(memory_space=pltpu.VMEM)
    scratch = (
        [
            pltpu.VMEM((4, row, 4 * DH), BF16),
            pltpu.VMEM((4, row, 4 * DH), BF16),
            pltpu.VMEM((8, row, 2 * DH), BF16),
            pltpu.VMEM((4, row, 2 * DH), BF16),
            pltpu.VMEM((2, 4) + piece, BF16),
        ]
        + sems(3) + sems(14) + sems(3)
        + [pltpu.VMEM(piece, BF16), pltpu.VMEM(piece, BF16)]
        + sems(1) + near_sum_scratch(piece) + spread_scratch()
    )
    operands = (length, embedded, own_rows, gain, weights, out_weight)
    specs = [pl.BlockSpec(memory_space=pltpu.SMEM)] + [vmem] * 5
    out = jax.ShapeDtypeStruct((2, 4) + piece, BF16)
    return call(functools.partial(self_kernel, width), ident, out, scratch, operands, specs)


def cross_kernel(width, length_ref, after_ref, gain_ref, weight_ref, out_ref, result_ref, *refs):
    blocks, got_y, ctx, got_ctx, terms, y_s, y_r, c_s, c_r, got_zh, zh_s, zh_r = refs[:12]
    near = refs[12:]
    half = near[3]
    y, zh = place_on(LINE_Y), place_on(LINE_ZH)
    v = lax.axis_index("vocab")
    side = peers_on(LINE_Y)
    devices = peers_on(LINE_CORE) + peers_on(LINE_X) + peers_on(LINE_ZH) + side
    barrier = greet(devices)
    row = after_ref.shape[0] // 2
    own = row // 4
    cols = 2 * DH
    share = pl.ds(pl.multiple_of((v // 2) * cols, cols), cols)
    for pair in range(2):
        wide = after_ref[pair * row : (pair + 1) * row].astype(F32)
        squares = jnp.sum(wide * wide, axis=-1, keepdims=True)
        scaled = (wide * gain_ref[...]).astype(BF16)
        for head in range(2):
            weight = weight_ref[:, head * 4 * DH + 2 * DH : (head + 1) * 4 * DH]
            product = jnp.dot(scaled, weight, preferred_element_type=F32)
            blocks[2 * pair + head, :row] = with_squares(product, squares, 0).astype(BF16)
        for k in range(4):
            lower = pair * row + k * own
            blocks[k, row + pair * own : row + (pair + 1) * own] = after_ref[lower : lower + own, share]
    pl.semaphore_wait(barrier, len(devices))
    copies = []
    for k in range(3):
        other = lax.rem(y + k + 1, 4)
        copies.append(send(blocks.at[other], got_y.at[y], side[k], y_s.at[k], y_r.at[k]))
    got_y[y] = blocks[y]
    for copy in copies:
        copy.wait()
    query = pltpu.roll(scaled_sum(got_y, row, 0, width), DH, 1)
    query = jnp.where(lanes_of(query.shape) < DH, query, 0.0).astype(BF16)
    both = weight_ref[:, 8 * DH :]
    visible = lanes_of((row, both.shape[0])) < length_ref[y // 2]
    ctx[...] = attend(query, both, visible, lax.rem(y, 2)).reshape(ctx.shape)
    copies = []
    for k in range(3):
        other = lax.rem(y + k + 1, 4)
        copies.append(send(ctx.at[other], got_ctx.at[y], side[k], c_s.at[k], c_r.at[k]))
    got_ctx[y] = ctx[y]
    for copy in copies:
        copy.wait()
    context = jnp.concatenate([got_ctx[0] + got_ctx[1], got_ctx[2] + got_ctx[3]], axis=0)
    out_cols = terms.shape[4]
    for core in range(2):
        for place in range(4):
            for far in range(2):
                lower = (far * 8 + place * 2 + core) * out_cols
                product = jnp.dot(context, out_ref[:, lower : lower + out_cols], preferred_element_type=F32)
                terms[core, place, far] = product.astype(BF16)
    near_sum(terms, *near)
    send(half.at[1 - zh], got_zh, peers_on(LINE_ZH)[0], zh_s.at[0], zh_r.at[0]).wait()
    total = half[zh].astype(F32) + got_zh[...].astype(F32)
    first = 2 * lax.rem(v, 2)
    for k in range(2):
        residual = got_y[first + k, row:].astype(F32)
        lanes = slice(k * cols, (k + 1) * cols)
        result_ref[:, lanes] = (residual + total[:, lanes]).astype(BF16)


def cross_block(ident, width, length, after, gain, weights, out_weight):
    row = after.shape[0] // 2
    own = row // 4
    block = (2, 2 * own, width // 16)
    vmem = pl.BlockSpec(memory_space=pltpu.VMEM)
    scratch = (
        [
            pltpu.VMEM((4, row + 2 * own, 2 * DH), BF16),
            pltpu.VMEM((4, row + 2 * own, 2 * DH), BF16),
            pltpu.VMEM((4, own, 2 * DH), BF16),
            pltpu.VMEM((4, own, 2 * DH), BF16),
            pltpu.VMEM((2, 4) + block, BF16),
        ]
        + sems(3) + sems(3) + [pltpu.VMEM(block[1:], BF16)] + sems(1) + near_sum_scratch(block)
    )
    operands = (length, after, gain, weights, out_weight)
    specs = [pl.BlockSpec(memory_space=pltpu.SMEM)] + [vmem] * 4
    out = jax.ShapeDtypeStruct(block[1:], BF16)
    return call(functools.partial(cross_kernel, width), ident, out, scratch, operands, specs)


def on_device(
    token_ids,
    keep_mask,
    target_length,
    source_length,
    embed_table,
    self_gain,
    query_weight,
    key_weight,
    value_weight,
    self_out_weight,
    cross_gain,
    cross_query_weight,
    cross_keys,
    cross_values,
    cross_out_weight,
):
    pairs, tokens = token_ids.shape
    vocab_index = lax.axis_index("vocab")
    y_index = place_on(LINE_Y)
    n_y, n_z = LINE_Y[1], LINE_Z[1]
    width = self_gain.shape[0]
    quarter = width // n_y
    cols = embed_table.shape[1]
    heads = 2
    row_tokens = pairs * n_y * tokens
    pieces = 8
    piece = row_tokens // pieces

    ids = jnp.where(keep_mask != 0, token_ids, -1).reshape(1, pairs * tokens)
    pos = cross_keys.shape[1]
    both = jnp.stack(
        [cross_keys.reshape(pairs, pos, heads, DH), cross_values.reshape(pairs, pos, heads, DH)], axis=3
    )
    both = both.transpose(0, 2, 1, 3, 4).reshape(n_y, pos, 2 * DH)
    out = (
        jax.ShapeDtypeStruct((n_z, n_y) + ids.shape, ids.dtype),
        jax.ShapeDtypeStruct(both.shape, BF16),
    )
    scratch = [pltpu.VMEM((n_y,) + ids.shape, ids.dtype), pltpu.SemaphoreType.DMA((3,))]
    ids, both = call(start_kernel, 0, out, scratch + sems(3) + sems(7) + sems(3), (ids, both))
    ids = ids.reshape(n_z, n_y, pairs, tokens).transpose(0, 2, 1, 3)
    ids = ids.reshape(n_z, pieces, piece).transpose(1, 0, 2).reshape(-1)

    weights = jnp.stack([key_weight, value_weight, query_weight, cross_query_weight], axis=1)
    weights = weights.reshape(cols, 4, heads, DH).transpose(0, 2, 1, 3).reshape(cols, heads * 4 * DH)
    weights = jnp.concatenate([weights, both.reshape(n_y * pos, 2 * DH)], axis=1)
    same_y = [[z * n_y + y for z in range(n_z)] for y in range(n_y)]
    weights = lax.all_gather(weights, "seq", axis_index_groups=same_y)
    weights = weights.reshape(n_z * cols, weights.shape[2])

    shard_rows = embed_table.shape[0]
    local_ids = ids - vocab_index * shard_rows
    inside = (local_ids >= 0) & (local_ids < shard_rows)
    picked = jnp.take(embed_table, jnp.clip(local_ids, 0, shard_rows - 1), axis=0)
    picked = jnp.where(inside[:, None], picked, jnp.zeros_like(picked))
    own_rows, embedded = embed_rows(picked.reshape(2, 4, n_z, piece, cols), 1)
    embedded = embedded.reshape(row_tokens, quarter)

    def quarter_of(values):
        part = values.reshape(-1, n_z, n_y, cols)
        return lax.dynamic_index_in_dim(part, y_index, 2, False).reshape(-1, quarter)

    out_part = quarter_of(self_out_weight)
    self_part, cross_part = quarter_of(self_gain), quarter_of(cross_gain)
    after = self_block(2, width, target_length, embedded, own_rows, self_part, weights, out_part)
    after = after.reshape(row_tokens, quarter)
    result = cross_block(3, width, source_length, after, cross_part, weights, cross_out_weight)
    return result.reshape(pairs, tokens, result.shape[1])


def solution(mesh):
    return jax.shard_map(
        on_device,
        mesh=mesh,
        in_specs=(
            P(None, "seq"),
            P(None, "seq"),
            P(),
            P(),
            P("vocab", "seq"),
            P(),
            P("seq", "vocab"),
            P("seq", "vocab"),
            P("seq", "vocab"),
            P("vocab", None),
            P(),
            P("seq", "vocab"),
            P(None, "seq", "vocab"),
            P(None, "seq", "vocab"),
            P("vocab", None),
        ),
        out_specs=P(None, "seq", "vocab"),
        check_vma=False,
    )
```

```python
import functools

import jax
import jax.numpy as jnp
from jax import lax
from jax.experimental import pallas as pl
from jax.experimental.pallas import tpu as pltpu
from jax.sharding import PartitionSpec as P

DH = 64
MESH = pl.DeviceIdType.MESH
F32 = jnp.float32
BF16 = jnp.bfloat16

LINE_Y = ("seq", 4, 1)
LINE_Z = ("seq", 8, 4)
LINE_CORE = ("vocab", 2, 1)
LINE_X = ("vocab", 4, 2)
LINE_ZH = ("vocab", 2, 8)


def place_on(line):
    axis, members, stride = line
    return lax.rem(lax.axis_index(axis) // stride, members)


def peer_of(line, shift):
    axis, members, stride = line
    here = lax.axis_index(axis)
    mine = lax.rem(here // stride, members)
    other = lax.rem(mine + shift, members)
    there = here + (other - mine) * stride
    if axis == "seq":
        return (lax.axis_index("vocab"), there), other
    return (there, lax.axis_index("seq")), other


def greet(devices):
    barrier = pltpu.get_barrier_semaphore()
    for target in devices:
        pl.semaphore_signal(barrier, inc=1, device_id=target, device_id_type=MESH)
    return barrier


def peers_on(line):
    return [peer_of(line, shift)[0] for shift in range(1, line[1])]


def send(source, target_ref, target, send_sem, recv_sem):
    copy = pltpu.make_async_remote_copy(
        src_ref=source,
        dst_ref=target_ref,
        send_sem=send_sem,
        recv_sem=recv_sem,
        device_id=target,
        device_id_type=MESH,
    )
    copy.start()
    return copy


def lanes_of(shape):
    return lax.broadcasted_iota(jnp.int32, shape, 1)


def by_head(left, right):
    low = lanes_of(left.shape) < DH
    return jnp.where(low, left, pltpu.roll(right, DH, 1)), jnp.where(low, pltpu.roll(left, DH, 1), right)


def quarter_of(ref):
    cols = ref.shape[1] // 32
    starts = [pl.multiple_of((4 * k + place_on(LINE_Y)) * cols, cols) for k in range(8)]
    return jnp.concatenate([ref[:, pl.ds(start, cols)] for start in starts], axis=1)


def start_kernel(ids_ref, keys_ref, values_ref, all_ids, both_out, row_ids, both_ref, own, y_s, y_r, z_s, z_r, b_s, b_r):
    y, z = place_on(LINE_Y), place_on(LINE_Z)
    near, far = peers_on(LINE_Y), peers_on(LINE_Z)
    barrier = greet(near + far)
    keep = pltpu.make_async_copy(ids_ref, row_ids.at[y], own.at[0])
    keep.start()
    for pair in range(2):
        first, second = by_head(keys_ref[pair].astype(F32), values_ref[pair].astype(F32))
        both_ref[2 * pair] = first.astype(BF16)
        both_ref[2 * pair + 1] = second.astype(BF16)
    both_out[y] = both_ref[y]
    pl.semaphore_wait(barrier, len(near + far))
    copies = [send(ids_ref, row_ids.at[y], near[k], y_s.at[k], y_r.at[k]) for k in range(3)]
    later = []
    for k in range(3):
        other = lax.rem(y + k + 1, 4)
        later.append(send(both_ref.at[other], both_out.at[y], near[k], b_s.at[k], b_r.at[k]))
    for copy in [keep] + copies:
        copy.wait()
    last = pltpu.make_async_copy(row_ids, all_ids.at[z], own.at[1])
    last.start()
    later += [send(row_ids, all_ids.at[z], far[k], z_s.at[k], z_r.at[k]) for k in range(7)]
    for copy in later + [last]:
        copy.wait()


def sems(count):
    return [pltpu.SemaphoreType.DMA((count,))] * 2


def call(kernel, ident, out, scratch, operands, in_specs=None):
    vmem = pl.BlockSpec(memory_space=pltpu.VMEM)
    return pl.pallas_call(
        kernel,
        out_shape=out,
        in_specs=in_specs or [vmem] * len(operands),
        out_specs=(vmem,) * len(out) if isinstance(out, tuple) else vmem,
        scratch_shapes=scratch,
        compiler_params=pltpu.CompilerParams(collective_id=ident, has_side_effects=True),
    )(*operands)


def near_sum(x_ref, got_core, part, got_x, half, core_s, core_r, x_s, x_r):
    core, place = place_on(LINE_CORE), place_on(LINE_X)
    twin, row = peers_on(LINE_CORE)[0], peers_on(LINE_X)
    order = (1, 2, 3, 0)
    core_copies = []
    for k, shift in enumerate(order):
        other = lax.rem(place + shift, 4)
        core_copies.append(send(x_ref.at[1 - core, other], got_core.at[other], twin, core_s.at[k], core_r.at[k]))
    x_copies = []
    for k, shift in enumerate(order):
        other = lax.rem(place + shift, 4)
        core_copies[k].wait()
        part[other] = (x_ref[core, other].astype(F32) + got_core[other].astype(F32)).astype(BF16)
        if shift:
            x_copies.append(send(part.at[other], got_x.at[k], row[k], x_s.at[k], x_r.at[k]))
    total = part[place].astype(F32)
    for k in range(3):
        x_copies[k].wait()
        total = total + got_x[k].astype(F32)
    half[...] = total.astype(BF16)


def near_sum_scratch(block):
    return [
        pltpu.VMEM((4,) + block, BF16),
        pltpu.VMEM((4,) + block, BF16),
        pltpu.VMEM((3,) + block, BF16),
        pltpu.VMEM(block, BF16),
    ] + sems(4) + sems(3)


def spread(block, all_ref, core_s, core_r, x_s, x_r, local):
    core, place = place_on(LINE_CORE), place_on(LINE_X)
    twin, row = peers_on(LINE_CORE)[0], peers_on(LINE_X)
    keep = pltpu.make_async_copy(block, all_ref.at[core, place], local)
    keep.start()
    copies = [send(block, all_ref.at[core, place], twin, core_s.at[0], core_r.at[0])]
    x_copies = [send(block, all_ref.at[core, place], row[k], x_s.at[k], x_r.at[k]) for k in range(3)]
    for k in range(3):
        x_copies[k].wait()
        source = all_ref.at[core, lax.rem(place + 3 - k, 4)]
        copies.append(send(source, source, twin, core_s.at[k + 1], core_r.at[k + 1]))
    for copy in copies:
        copy.wait()
    keep.wait()


def spread_scratch():
    return sems(4) + sems(3) + [pltpu.SemaphoreType.DMA]


def rows_kernel(x_ref, both_ref, own_ref, all_ref, all_both, *refs):
    near, refs = refs[:8], refs[8:]
    got, z_s, z_r, zh_s, zh_r, b_s, b_r = refs[:7]
    half = near[3]
    z, zh = place_on(LINE_Z), place_on(LINE_ZH)
    v, s = lax.axis_index("vocab"), lax.axis_index("seq")
    level = peers_on(LINE_Z)
    over_v = peer_of(LINE_ZH, 1)[0][0]
    across = [(over_v, peer_of(LINE_Z, k)[0][1]) for k in range(8)]
    devices = peers_on(LINE_CORE) + peers_on(LINE_X) + level + across
    barrier = greet(devices)
    pl.semaphore_wait(barrier, len(devices))
    late = [send(both_ref, all_both.at[z], level[k], b_s.at[k], b_r.at[k]) for k in range(7)]
    all_both[z] = both_ref[...]
    near_sum(x_ref, *near)
    copies = []
    for k in (4, 3, 5, 2, 6, 1, 7, 0):
        other = lax.rem(z + k, 8)
        copies.append(send(half.at[other], got.at[zh, z], across[k], zh_s.at[k], zh_r.at[k]))
        if k:
            copies.append(send(half.at[other], got.at[zh, z], level[k - 1], z_s.at[k - 1], z_r.at[k - 1]))
    got[zh, z] = half[z]
    for copy in copies:
        copy.wait()
    cols = got.shape[3]
    for k in range(8):
        own_ref[:, k * cols : (k + 1) * cols] = (got[0, k].astype(F32) + got[1, k].astype(F32)).astype(BF16)
    spread(own_ref, all_ref, *refs[7:])
    for copy in late:
        copy.wait()


def embed_rows(x, both, ident):
    block = x.shape[2:]
    own = (block[1], block[0] * block[2])
    out = tuple(jax.ShapeDtypeStruct(shape, BF16) for shape in (own, (2, 4) + own, (8,) + both.shape))
    scratch = near_sum_scratch(block) + [pltpu.VMEM((2,) + block, BF16)]
    scratch += sems(7) + sems(8) + sems(7) + spread_scratch()
    return call(rows_kernel, ident, out, scratch, (x, both))


def with_squares(product, squares, lane):
    high = squares.astype(BF16).astype(F32)
    at = lanes_of(product.shape)
    return jnp.where(at == lane, high, jnp.where(at == lane + 1, squares - high, product))


def scaled_sum(got, rows, lane, width):
    total = got[0, :rows].astype(F32)
    for k in range(1, 4):
        total = total + got[k, :rows].astype(F32)
    squares = total[:, lane : lane + 1] + total[:, lane + 1 : lane + 2]
    return total * lax.rsqrt(squares / width + 1e-06)


def attend(query, both, visible, head):
    scores = lax.dot_general(query, both, (((1,), (1,)), ((), ())), preferred_element_type=F32)
    scores = jnp.where(visible, scores, -jnp.inf)
    raised = jnp.exp(scores - jnp.max(scores, axis=-1, keepdims=True))
    totals = jnp.sum(raised, axis=-1, keepdims=True)
    mixed = jnp.dot(raised.astype(BF16), both, preferred_element_type=F32) / totals
    moved = jnp.where(head == 0, pltpu.roll(mixed, DH, 1), mixed)
    return jnp.where(lanes_of(moved.shape) // DH == head, moved, 0.0).astype(BF16)


def self_kernel(width, length_ref, emb_ref, own_ref, gain_ref, weight_ref, out_ref, all_ref, *refs):
    blocks, got_y, kv, got_ctx, terms, y_s, y_r, up_s, up_r, c_s, c_r, got_zh, piece, zh_s, zh_r = refs[:15]
    near, far = refs[15:23], refs[23:]
    half = near[3]
    y, z = place_on(LINE_Y), place_on(LINE_Z)
    side = peers_on(LINE_Y)
    up, down = peer_of(LINE_Z, 1)[0], peer_of(LINE_Z, 7)[0]
    has_up, has_down = z < 7, z > 0
    devices = peers_on(LINE_CORE) + peers_on(LINE_X) + peers_on(LINE_ZH) + side
    barrier = greet(devices)

    @pl.when(has_up)
    def _():
        pl.semaphore_signal(barrier, inc=1, device_id=up, device_id_type=MESH)

    @pl.when(has_down)
    def _():
        pl.semaphore_signal(barrier, inc=1, device_id=down, device_id_type=MESH)

    row, quarter = emb_ref.shape[0] // 2, emb_ref.shape[1]
    gain = quarter_of(gain_ref)
    weights = [weight_ref[:, k].reshape(quarter, 2 * DH) for k in range(3)]
    for pair in range(2):
        wide = emb_ref[pair * row : (pair + 1) * row].astype(F32)
        squares = jnp.sum(wide * wide, axis=-1, keepdims=True)
        scaled = (wide * gain).astype(BF16)
        keys, values, queries = (jnp.dot(scaled, weight, preferred_element_type=F32) for weight in weights)
        kv_heads = by_head(keys, values)
        q_heads = (queries, pltpu.roll(queries, DH, 1))
        for head in range(2):
            blocks[2 * pair + head, :, : 2 * DH] = kv_heads[head].astype(BF16)
            blocks[2 * pair + head, :, 2 * DH :] = with_squares(q_heads[head], squares, DH).astype(BF16)
    for k in range(1, 8):

        @pl.when(k > z)
        def _():
            kv[k] = jnp.zeros(kv.shape[1:], BF16)

    @pl.when(has_up & has_down)
    def _():
        pl.semaphore_wait(barrier, len(devices) + 2)

    @pl.when(jnp.logical_not(has_up & has_down))
    def _():
        pl.semaphore_wait(barrier, len(devices) + 1)

    copies = []
    for k in range(3):
        other = lax.rem(y + k + 1, 4)
        copies.append(send(blocks.at[other], got_y.at[y], side[k], y_s.at[k], y_r.at[k]))
    got_y[y] = blocks[y]
    for copy in copies:
        copy.wait()
    qkv = scaled_sum(got_y, row, 3 * DH, width)
    kv[z] = qkv[:, : 2 * DH].astype(BF16)
    query = qkv[:, 2 * DH :]
    query = jnp.where(lanes_of(query.shape) < DH, query, 0.0).astype(BF16)

    chunk = row // 2

    def passing(source, step, part):
        place = kv.at[source, part * chunk : (part + 1) * chunk]
        index = (step - 1) * 2 + part
        return pltpu.make_async_remote_copy(
            src_ref=place,
            dst_ref=place,
            send_sem=up_s.at[index],
            recv_sem=up_r.at[index],
            device_id=up,
            device_id_type=MESH,
        )

    for step in range(1, 9):
        for part in range(2):
            if step > 1:

                @pl.when(z - step + 1 >= 0)
                def _():
                    passing(z - step + 1, step - 1, part).wait_recv()

            if step < 8:

                @pl.when(has_up & (z - step + 1 >= 0))
                def _():
                    passing(z - step + 1, step, part).start()

    pair = y // 2
    both = kv[...].reshape(8 * row, 2 * DH)
    key_pos = lanes_of((row, 8 * row))
    query_pos = z * row + lax.broadcasted_iota(jnp.int32, (row, 8 * row), 0)
    visible = (key_pos <= query_pos) & (key_pos < length_ref[pair])
    got_ctx[y] = attend(query, both, visible, lax.rem(y, 2))
    copies = [send(got_ctx.at[y], got_ctx.at[y], side[k], c_s.at[k], c_r.at[k]) for k in range(3)]
    for step in range(1, 8):
        for part in range(2):

            @pl.when(has_up & (z - step + 1 >= 0))
            def _():
                passing(z - step + 1, step, part).wait_send()

    for copy in copies:
        copy.wait()
    out_part = quarter_of(out_ref)
    for pair in range(2):
        context = got_ctx[2 * pair] + got_ctx[2 * pair + 1]
        product = jnp.dot(context, out_part, preferred_element_type=F32).astype(BF16)
        terms[pair] = product.reshape(terms.shape[1:])
    near_sum(terms, *near)
    send(half, got_zh, peers_on(LINE_ZH)[0], zh_s.at[0], zh_r.at[0]).wait()
    piece[...] = (own_ref[...].astype(F32) + (half[...].astype(F32) + got_zh[...].astype(F32))).astype(BF16)
    spread(piece, all_ref, *far)


def self_block(ident, width, length, embedded, own_rows, gain, weights, out_weight):
    tokens, quarter = embedded.shape
    row = tokens // 2
    piece = own_rows.shape
    vmem = pl.BlockSpec(memory_space=pltpu.VMEM)
    scratch = (
        [
            pltpu.VMEM((4, row, 4 * DH), BF16),
            pltpu.VMEM((4, row, 4 * DH), BF16),
            pltpu.VMEM((8, row, 2 * DH), BF16),
            pltpu.VMEM((4, row, 2 * DH), BF16),
            pltpu.VMEM((2, 4) + piece, BF16),
        ]
        + sems(3) + sems(14) + sems(3)
        + [pltpu.VMEM(piece, BF16), pltpu.VMEM(piece, BF16)]
        + sems(1) + near_sum_scratch(piece) + spread_scratch()
    )
    operands = (length, embedded, own_rows, gain, weights, out_weight)
    specs = [pl.BlockSpec(memory_space=pltpu.SMEM)] + [vmem] * 5
    out = jax.ShapeDtypeStruct((2, 4) + piece, BF16)
    return call(functools.partial(self_kernel, width), ident, out, scratch, operands, specs)


def cross_kernel(width, length_ref, after_ref, gain_ref, weight_ref, both_ref, out_ref, result_ref, *refs):
    blocks, got_y, ctx, got_ctx, terms, y_s, y_r, c_s, c_r, got_zh, zh_s, zh_r = refs[:12]
    near = refs[12:]
    half = near[3]
    y, zh = place_on(LINE_Y), place_on(LINE_ZH)
    v = lax.axis_index("vocab")
    side = peers_on(LINE_Y)
    devices = peers_on(LINE_CORE) + peers_on(LINE_X) + peers_on(LINE_ZH) + side
    barrier = greet(devices)
    row = after_ref.shape[0] // 2
    own = row // 4
    cols = 2 * DH
    gain = quarter_of(gain_ref)
    weight = weight_ref[:, 3].reshape(after_ref.shape[1], 2 * DH)
    share = pl.ds(pl.multiple_of((v // 2) * cols, cols), cols)
    for pair in range(2):
        wide = after_ref[pair * row : (pair + 1) * row].astype(F32)
        squares = jnp.sum(wide * wide, axis=-1, keepdims=True)
        scaled = (wide * gain).astype(BF16)
        product = jnp.dot(scaled, weight, preferred_element_type=F32)
        for head in range(2):
            queries = pltpu.roll(product, DH, 1) if head else product
            blocks[2 * pair + head, :row] = with_squares(queries, squares, DH).astype(BF16)
        for k in range(4):
            lower = pair * row + k * own
            blocks[k, row + pair * own : row + (pair + 1) * own] = after_ref[lower : lower + own, share]
    pl.semaphore_wait(barrier, len(devices))
    copies = []
    for k in range(3):
        other = lax.rem(y + k + 1, 4)
        copies.append(send(blocks.at[other], got_y.at[y], side[k], y_s.at[k], y_r.at[k]))
    got_y[y] = blocks[y]
    for copy in copies:
        copy.wait()
    query = scaled_sum(got_y, row, DH, width)
    query = jnp.where(lanes_of(query.shape) < DH, query, 0.0).astype(BF16)
    both = both_ref[...]
    visible = lanes_of((row, both.shape[0])) < length_ref[y // 2]
    ctx[...] = attend(query, both, visible, lax.rem(y, 2)).reshape(ctx.shape)
    copies = []
    for k in range(3):
        other = lax.rem(y + k + 1, 4)
        copies.append(send(ctx.at[other], got_ctx.at[y], side[k], c_s.at[k], c_r.at[k]))
    got_ctx[y] = ctx[y]
    for copy in copies:
        copy.wait()
    context = jnp.concatenate([got_ctx[0] + got_ctx[1], got_ctx[2] + got_ctx[3]], axis=0)
    out_cols = terms.shape[4]
    for core in range(2):
        for place in range(4):
            for far in range(2):
                lower = (far * 8 + place * 2 + core) * out_cols
                product = jnp.dot(context, out_ref[:, lower : lower + out_cols], preferred_element_type=F32)
                terms[core, place, far] = product.astype(BF16)
    near_sum(terms, *near)
    send(half.at[1 - zh], got_zh, peers_on(LINE_ZH)[0], zh_s.at[0], zh_r.at[0]).wait()
    total = half[zh].astype(F32) + got_zh[...].astype(F32)
    first = 2 * lax.rem(v, 2)
    for k in range(2):
        residual = got_y[first + k, row:].astype(F32)
        lanes = slice(k * cols, (k + 1) * cols)
        result_ref[:, lanes] = (residual + total[:, lanes]).astype(BF16)


def cross_block(ident, width, length, after, gain, weights, both, out_weight):
    row = after.shape[0] // 2
    own = row // 4
    block = (2, 2 * own, width // 16)
    vmem = pl.BlockSpec(memory_space=pltpu.VMEM)
    scratch = (
        [
            pltpu.VMEM((4, row + 2 * own, 2 * DH), BF16),
            pltpu.VMEM((4, row + 2 * own, 2 * DH), BF16),
            pltpu.VMEM((4, own, 2 * DH), BF16),
            pltpu.VMEM((4, own, 2 * DH), BF16),
            pltpu.VMEM((2, 4) + block, BF16),
        ]
        + sems(3) + sems(3) + [pltpu.VMEM(block[1:], BF16)] + sems(1) + near_sum_scratch(block)
    )
    operands = (length, after, gain, weights, both, out_weight)
    specs = [pl.BlockSpec(memory_space=pltpu.SMEM)] + [vmem] * 5
    out = jax.ShapeDtypeStruct(block[1:], BF16)
    return call(functools.partial(cross_kernel, width), ident, out, scratch, operands, specs)


def on_device(
    token_ids,
    keep_mask,
    target_length,
    source_length,
    embed_table,
    self_gain,
    query_weight,
    key_weight,
    value_weight,
    self_out_weight,
    cross_gain,
    cross_query_weight,
    cross_keys,
    cross_values,
    cross_out_weight,
):
    pairs, tokens = token_ids.shape
    vocab_index = lax.axis_index("vocab")
    n_y, n_z = LINE_Y[1], LINE_Z[1]
    width = self_gain.shape[0]
    quarter = width // n_y
    cols = embed_table.shape[1]
    row_tokens = pairs * n_y * tokens
    pieces = 8
    piece = row_tokens // pieces

    same_y = [[z * n_y + y for z in range(n_z)] for y in range(n_y)]
    weights = jnp.stack([key_weight, value_weight, query_weight, cross_query_weight])
    weights = lax.all_gather(weights, "seq", axis_index_groups=same_y)

    ids = jnp.where(keep_mask != 0, token_ids, -1).reshape(1, pairs * tokens)
    both_shape = (n_y, cross_keys.shape[1], 2 * DH)
    out = (
        jax.ShapeDtypeStruct((n_z, n_y) + ids.shape, ids.dtype),
        jax.ShapeDtypeStruct(both_shape, BF16),
    )
    scratch = [
        pltpu.VMEM((n_y,) + ids.shape, ids.dtype),
        pltpu.VMEM(both_shape, BF16),
        pltpu.SemaphoreType.DMA((2,)),
    ]
    operands = (ids, cross_keys, cross_values)
    ids, both = call(start_kernel, 0, out, scratch + sems(3) + sems(7) + sems(3), operands)
    ids = ids.reshape(n_z, n_y, pairs, tokens).transpose(0, 2, 1, 3)
    ids = ids.reshape(n_z, pieces, piece).transpose(1, 0, 2).reshape(-1)

    shard_rows = embed_table.shape[0]
    local_ids = ids - vocab_index * shard_rows
    inside = (local_ids >= 0) & (local_ids < shard_rows)
    picked = jnp.take(embed_table, jnp.clip(local_ids, 0, shard_rows - 1), axis=0)
    picked = jnp.where(inside[:, None], picked, jnp.zeros_like(picked))
    own_rows, embedded, both = embed_rows(picked.reshape(2, 4, n_z, piece, cols), both, 1)
    both = both.reshape(-1, 2 * DH)
    embedded = embedded.reshape(row_tokens, quarter)

    gains = [gain.reshape(1, width) for gain in (self_gain, cross_gain)]
    after = self_block(2, width, target_length, embedded, own_rows, gains[0], weights, self_out_weight)
    after = after.reshape(row_tokens, quarter)
    result = cross_block(3, width, source_length, after, gains[1], weights, both, cross_out_weight)
    return result.reshape(pairs, tokens, result.shape[1])


def solution(mesh):
    return jax.shard_map(
        on_device,
        mesh=mesh,
        in_specs=(
            P(None, "seq"),
            P(None, "seq"),
            P(),
            P(),
            P("vocab", "seq"),
            P(),
            P("seq", "vocab"),
            P("seq", "vocab"),
            P("seq", "vocab"),
            P("vocab", None),
            P(),
            P("seq", "vocab"),
            P(None, "seq", "vocab"),
            P(None, "seq", "vocab"),
            P("vocab", None),
        ),
        out_specs=P(None, "seq", "vocab"),
        check_vma=False,
    )
```

```python
import functools

import jax
import jax.numpy as jnp
from jax import lax
from jax.experimental import pallas as pl
from jax.experimental.pallas import tpu as pltpu
from jax.sharding import PartitionSpec as P

DH = 64
MESH = pl.DeviceIdType.MESH
F32 = jnp.float32
BF16 = jnp.bfloat16

LINE_Y = ("seq", 4, 1)
LINE_Z = ("seq", 8, 4)
LINE_CORE = ("vocab", 2, 1)
LINE_X = ("vocab", 4, 2)
LINE_ZH = ("vocab", 2, 8)


def place_on(line):
    axis, members, stride = line
    return lax.rem(lax.axis_index(axis) // stride, members)


def peer_of(line, shift):
    axis, members, stride = line
    here = lax.axis_index(axis)
    mine = lax.rem(here // stride, members)
    other = lax.rem(mine + shift, members)
    there = here + (other - mine) * stride
    if axis == "seq":
        return (lax.axis_index("vocab"), there), other
    return (there, lax.axis_index("seq")), other


def greet(devices):
    barrier = pltpu.get_barrier_semaphore()
    for target in devices:
        pl.semaphore_signal(barrier, inc=1, device_id=target, device_id_type=MESH)
    return barrier


def peers_on(line):
    return [peer_of(line, shift)[0] for shift in range(1, line[1])]


def send(source, target_ref, target, send_sem, recv_sem):
    copy = pltpu.make_async_remote_copy(
        src_ref=source,
        dst_ref=target_ref,
        send_sem=send_sem,
        recv_sem=recv_sem,
        device_id=target,
        device_id_type=MESH,
    )
    copy.start()
    return copy


def lanes_of(shape):
    return lax.broadcasted_iota(jnp.int32, shape, 1)


def by_head(left, right):
    low = lanes_of(left.shape) < DH
    return jnp.where(low, left, pltpu.roll(right, DH, 1)), jnp.where(low, pltpu.roll(left, DH, 1), right)


def quarter_of(ref):
    cols = ref.shape[1] // 32
    starts = [pl.multiple_of((4 * k + place_on(LINE_Y)) * cols, cols) for k in range(8)]
    return jnp.concatenate([ref[:, pl.ds(start, cols)] for start in starts], axis=1)


def start_kernel(ids_ref, keys_ref, values_ref, all_ids, both_out, row_ids, both_ref, own, y_s, y_r, z_s, z_r, b_s, b_r):
    y, z = place_on(LINE_Y), place_on(LINE_Z)
    near, far = peers_on(LINE_Y), peers_on(LINE_Z)
    barrier = greet(near + far)
    keep = pltpu.make_async_copy(ids_ref, row_ids.at[y], own.at[0])
    keep.start()
    for pair in range(2):
        first, second = by_head(keys_ref[pair].astype(F32), values_ref[pair].astype(F32))
        both_ref[2 * pair] = first.astype(BF16)
        both_ref[2 * pair + 1] = second.astype(BF16)
    both_out[y] = both_ref[y]
    pl.semaphore_wait(barrier, len(near + far))
    copies = [send(ids_ref, row_ids.at[y], near[k], y_s.at[k], y_r.at[k]) for k in range(3)]
    later = []
    for k in range(3):
        other = lax.rem(y + k + 1, 4)
        later.append(send(both_ref.at[other], both_out.at[y], near[k], b_s.at[k], b_r.at[k]))
    for copy in [keep] + copies:
        copy.wait()
    last = pltpu.make_async_copy(row_ids, all_ids.at[z], own.at[1])
    last.start()
    later += [send(row_ids, all_ids.at[z], far[k], z_s.at[k], z_r.at[k]) for k in range(7)]
    for copy in later + [last]:
        copy.wait()


def sems(count):
    return [pltpu.SemaphoreType.DMA((count,))] * 2


def call(kernel, ident, out, scratch, operands, in_specs=None):
    vmem = pl.BlockSpec(memory_space=pltpu.VMEM)
    return pl.pallas_call(
        kernel,
        out_shape=out,
        in_specs=in_specs or [vmem] * len(operands),
        out_specs=(vmem,) * len(out) if isinstance(out, tuple) else vmem,
        scratch_shapes=scratch,
        compiler_params=pltpu.CompilerParams(collective_id=ident, has_side_effects=True),
    )(*operands)


def half_pair(block):
    return pltpu.VMEM((2, block[0] // 2) + tuple(block[1:]), BF16)


def ring_far(line, source, relay, send_sem, recv_sem):
    right, left = peer_of(line, 1)[0], peer_of(line, 3)[0]
    rows = relay.shape[1]
    return [
        send(source.at[:rows], relay.at[0], right, send_sem.at[0], recv_sem.at[0]),
        send(source.at[rows:], relay.at[1], left, send_sem.at[1], recv_sem.at[1]),
    ]


def ring_forward(line, far, relay, to_right, to_left, send_sem, recv_sem):
    right, left = peer_of(line, 1)[0], peer_of(line, 3)[0]
    far[0].wait()
    first = send(relay.at[0], to_right, right, send_sem.at[4], recv_sem.at[4])
    far[1].wait()
    return [first, send(relay.at[1], to_left, left, send_sem.at[5], recv_sem.at[5])]


def exchange_y(blocks, got, relay, send_sem, recv_sem):
    y = place_on(LINE_Y)
    before, behind = lax.rem(y + 3, 4), lax.rem(y + 1, 4)
    right, left = peer_of(LINE_Y, 1)[0], peer_of(LINE_Y, 3)[0]
    far = ring_far(LINE_Y, blocks.at[lax.rem(y + 2, 4)], relay, send_sem, recv_sem)
    copies = [
        send(blocks.at[behind], got.at[y], right, send_sem.at[2], recv_sem.at[2]),
        send(blocks.at[before], got.at[y], left, send_sem.at[3], recv_sem.at[3]),
    ]
    got[y] = blocks[y]
    rows = relay.shape[1]
    copies += ring_forward(LINE_Y, far, relay, got.at[before, :rows], got.at[behind, rows:], send_sem, recv_sem)
    for copy in copies:
        copy.wait()


def near_sum(x_ref, got_core, part, got_x, half, relay, core_s, core_r, x_s, x_r):
    core, place = place_on(LINE_CORE), place_on(LINE_X)
    twin, row = peers_on(LINE_CORE)[0], peers_on(LINE_X)
    order = (2, 1, 3, 0)
    core_copies = []
    for k, shift in enumerate(order):
        other = lax.rem(place + shift, 4)
        core_copies.append(send(x_ref.at[1 - core, other], got_core.at[other], twin, core_s.at[k], core_r.at[k]))
    copies = []
    for k, shift in enumerate(order):
        other = lax.rem(place + shift, 4)
        core_copies[k].wait()
        part[other] = (x_ref[core, other].astype(F32) + got_core[other].astype(F32)).astype(BF16)
        if shift == 2:
            far = ring_far(LINE_X, part.at[other], relay, x_s, x_r)
        elif shift:
            copies.append(send(part.at[other], got_x.at[shift - 1], row[shift - 1], x_s.at[k + 1], x_r.at[k + 1]))
    half_rows = relay.shape[1]
    copies += ring_forward(LINE_X, far, relay, got_x.at[1, :half_rows], got_x.at[1, half_rows:], x_s, x_r)
    total = part[place].astype(F32)
    for copy in copies:
        copy.wait()
    for k in range(3):
        total = total + got_x[k].astype(F32)
    half[...] = total.astype(BF16)


def near_sum_scratch(block):
    return [
        pltpu.VMEM((4,) + block, BF16),
        pltpu.VMEM((4,) + block, BF16),
        pltpu.VMEM((3,) + block, BF16),
        pltpu.VMEM(block, BF16),
        half_pair(block),
    ] + sems(4) + sems(6)


def spread(block, all_ref, core_s, core_r, x_s, x_r, local):
    core, place = place_on(LINE_CORE), place_on(LINE_X)
    twin, row = peers_on(LINE_CORE)[0], peers_on(LINE_X)
    keep = pltpu.make_async_copy(block, all_ref.at[core, place], local)
    keep.start()
    copies = [send(block, all_ref.at[core, place], twin, core_s.at[0], core_r.at[0])]
    right, left = row[0], row[2]
    rows = block.shape[0] // 2
    upper, lower = slice(0, rows), slice(rows, 2 * rows)

    def pass_on(source, member, part, target, k):
        return send(source, all_ref.at[core, member, part], target, x_s.at[k], x_r.at[k])

    first = pass_on(block.at[upper], place, upper, right, 0)
    second = pass_on(block.at[lower], place, lower, left, 1)
    from_left = pass_on(block.at[lower], place, lower, right, 2)
    from_right = pass_on(block.at[upper], place, upper, left, 3)
    before, behind = lax.rem(place + 3, 4), lax.rem(place + 1, 4)
    first.wait()
    far = [pass_on(all_ref.at[core, before, upper], before, upper, right, 4)]
    second.wait()
    far.append(pass_on(all_ref.at[core, behind, lower], behind, lower, left, 5))
    for k, (member, needs) in enumerate(
        ((before, [from_left]), (behind, [from_right]), (lax.rem(place + 2, 4), far))
    ):
        for copy in needs:
            copy.wait()
        whole = all_ref.at[core, member]
        copies.append(send(whole, whole, twin, core_s.at[k + 1], core_r.at[k + 1]))
    for copy in copies:
        copy.wait()
    keep.wait()


def spread_scratch():
    return sems(4) + sems(6) + [pltpu.SemaphoreType.DMA]


def rows_kernel(x_ref, both_ref, own_ref, all_ref, all_both, *refs):
    near, refs = refs[:9], refs[9:]
    got, z_s, z_r, zh_s, zh_r, b_s, b_r = refs[:7]
    half = near[3]
    z, zh = place_on(LINE_Z), place_on(LINE_ZH)
    v, s = lax.axis_index("vocab"), lax.axis_index("seq")
    level = peers_on(LINE_Z)
    over_v = peer_of(LINE_ZH, 1)[0][0]
    across = [(over_v, peer_of(LINE_Z, k)[0][1]) for k in range(8)]
    devices = peers_on(LINE_CORE) + peers_on(LINE_X) + level + across
    barrier = greet(devices)
    pl.semaphore_wait(barrier, len(devices))
    late = [send(both_ref, all_both.at[z], level[k], b_s.at[k], b_r.at[k]) for k in range(7)]
    all_both[z] = both_ref[...]
    near_sum(x_ref, *near)
    copies = []
    for k in (4, 3, 5, 2, 6, 1, 7, 0):
        other = lax.rem(z + k, 8)
        copies.append(send(half.at[other], got.at[zh, z], across[k], zh_s.at[k], zh_r.at[k]))
        if k:
            copies.append(send(half.at[other], got.at[zh, z], level[k - 1], z_s.at[k - 1], z_r.at[k - 1]))
    got[zh, z] = half[z]
    for copy in copies:
        copy.wait()
    cols = got.shape[3]
    for k in range(8):
        own_ref[:, k * cols : (k + 1) * cols] = (got[0, k].astype(F32) + got[1, k].astype(F32)).astype(BF16)
    spread(own_ref, all_ref, *refs[7:])
    for copy in late:
        copy.wait()


def embed_rows(x, both, ident):
    block = x.shape[2:]
    own = (block[1], block[0] * block[2])
    out = tuple(jax.ShapeDtypeStruct(shape, BF16) for shape in (own, (2, 4) + own, (8,) + both.shape))
    scratch = near_sum_scratch(block) + [pltpu.VMEM((2,) + block, BF16)]
    scratch += sems(7) + sems(8) + sems(7) + spread_scratch()
    return call(rows_kernel, ident, out, scratch, (x, both))


def with_squares(product, squares, lane):
    high = squares.astype(BF16).astype(F32)
    at = lanes_of(product.shape)
    return jnp.where(at == lane, high, jnp.where(at == lane + 1, squares - high, product))


def scaled_sum(got, rows, lane, width):
    total = got[0, :rows].astype(F32)
    for k in range(1, 4):
        total = total + got[k, :rows].astype(F32)
    squares = total[:, lane : lane + 1] + total[:, lane + 1 : lane + 2]
    return total * lax.rsqrt(squares / width + 1e-06)


def attend(query, both, visible, head):
    scores = lax.dot_general(query, both, (((1,), (1,)), ((), ())), preferred_element_type=F32)
    scores = jnp.where(visible, scores, -jnp.inf)
    raised = jnp.exp(scores - jnp.max(scores, axis=-1, keepdims=True))
    totals = jnp.sum(raised, axis=-1, keepdims=True)
    mixed = jnp.dot(raised.astype(BF16), both, preferred_element_type=F32) / totals
    moved = jnp.where(head == 0, pltpu.roll(mixed, DH, 1), mixed)
    return jnp.where(lanes_of(moved.shape) // DH == head, moved, 0.0).astype(BF16)


def self_kernel(width, length_ref, emb_ref, own_ref, gain_ref, weight_ref, out_ref, all_ref, *refs):
    blocks, got_y, kv, got_ctx, terms, y_s, y_r, up_s, up_r, c_s, c_r, got_zh, piece, zh_s, zh_r, relay = refs[:16]
    near, far = refs[16:25], refs[25:]
    half = near[3]
    y, z = place_on(LINE_Y), place_on(LINE_Z)
    side = peers_on(LINE_Y)
    up, down = peer_of(LINE_Z, 1)[0], peer_of(LINE_Z, 7)[0]
    has_up, has_down = z < 7, z > 0
    devices = peers_on(LINE_CORE) + peers_on(LINE_X) + peers_on(LINE_ZH) + side
    barrier = greet(devices)

    @pl.when(has_up)
    def _():
        pl.semaphore_signal(barrier, inc=1, device_id=up, device_id_type=MESH)

    @pl.when(has_down)
    def _():
        pl.semaphore_signal(barrier, inc=1, device_id=down, device_id_type=MESH)

    row, quarter = emb_ref.shape[0] // 2, emb_ref.shape[1]
    gain = quarter_of(gain_ref)
    weights = [weight_ref[:, k].reshape(quarter, 2 * DH) for k in range(3)]
    for pair in range(2):
        wide = emb_ref[pair * row : (pair + 1) * row].astype(F32)
        squares = jnp.sum(wide * wide, axis=-1, keepdims=True)
        scaled = (wide * gain).astype(BF16)
        keys, values, queries = (jnp.dot(scaled, weight, preferred_element_type=F32) for weight in weights)
        kv_heads = by_head(keys, values)
        q_heads = (queries, pltpu.roll(queries, DH, 1))
        for head in range(2):
            blocks[2 * pair + head, :, : 2 * DH] = kv_heads[head].astype(BF16)
            blocks[2 * pair + head, :, 2 * DH :] = with_squares(q_heads[head], squares, DH).astype(BF16)
    for k in range(1, 8):

        @pl.when(k > z)
        def _():
            kv[k] = jnp.zeros(kv.shape[1:], BF16)

    @pl.when(has_up & has_down)
    def _():
        pl.semaphore_wait(barrier, len(devices) + 2)

    @pl.when(jnp.logical_not(has_up & has_down))
    def _():
        pl.semaphore_wait(barrier, len(devices) + 1)

    exchange_y(blocks, got_y, relay, y_s, y_r)
    qkv = scaled_sum(got_y, row, 3 * DH, width)
    kv[z] = qkv[:, : 2 * DH].astype(BF16)
    query = qkv[:, 2 * DH :]
    query = jnp.where(lanes_of(query.shape) < DH, query, 0.0).astype(BF16)

    chunk = row // 2

    def passing(source, step, part):
        place = kv.at[source, part * chunk : (part + 1) * chunk]
        index = (step - 1) * 2 + part
        return pltpu.make_async_remote_copy(
            src_ref=place,
            dst_ref=place,
            send_sem=up_s.at[index],
            recv_sem=up_r.at[index],
            device_id=up,
            device_id_type=MESH,
        )

    for step in range(1, 9):
        for part in range(2):
            if step > 1:

                @pl.when(z - step + 1 >= 0)
                def _():
                    passing(z - step + 1, step - 1, part).wait_recv()

            if step < 8:

                @pl.when(has_up & (z - step + 1 >= 0))
                def _():
                    passing(z - step + 1, step, part).start()

    pair = y // 2
    both = kv[...].reshape(8 * row, 2 * DH)
    key_pos = lanes_of((row, 8 * row))
    query_pos = z * row + lax.broadcasted_iota(jnp.int32, (row, 8 * row), 0)
    visible = (key_pos <= query_pos) & (key_pos < length_ref[pair])
    got_ctx[y] = attend(query, both, visible, lax.rem(y, 2))
    copies = [send(got_ctx.at[y], got_ctx.at[y], side[k], c_s.at[k], c_r.at[k]) for k in range(3)]
    for step in range(1, 8):
        for part in range(2):

            @pl.when(has_up & (z - step + 1 >= 0))
            def _():
                passing(z - step + 1, step, part).wait_send()

    for copy in copies:
        copy.wait()
    out_part = quarter_of(out_ref)
    for pair in range(2):
        context = got_ctx[2 * pair] + got_ctx[2 * pair + 1]
        product = jnp.dot(context, out_part, preferred_element_type=F32).astype(BF16)
        terms[pair] = product.reshape(terms.shape[1:])
    near_sum(terms, *near)
    send(half, got_zh, peers_on(LINE_ZH)[0], zh_s.at[0], zh_r.at[0]).wait()
    piece[...] = (own_ref[...].astype(F32) + (half[...].astype(F32) + got_zh[...].astype(F32))).astype(BF16)
    spread(piece, all_ref, *far)


def self_block(ident, width, length, embedded, own_rows, gain, weights, out_weight):
    tokens, quarter = embedded.shape
    row = tokens // 2
    piece = own_rows.shape
    vmem = pl.BlockSpec(memory_space=pltpu.VMEM)
    scratch = (
        [
            pltpu.VMEM((4, row, 4 * DH), BF16),
            pltpu.VMEM((4, row, 4 * DH), BF16),
            pltpu.VMEM((8, row, 2 * DH), BF16),
            pltpu.VMEM((4, row, 2 * DH), BF16),
            pltpu.VMEM((2, 4) + piece, BF16),
        ]
        + sems(6) + sems(14) + sems(3)
        + [pltpu.VMEM(piece, BF16), pltpu.VMEM(piece, BF16)]
        + sems(1) + [half_pair((row, 4 * DH))] + near_sum_scratch(piece) + spread_scratch()
    )
    operands = (length, embedded, own_rows, gain, weights, out_weight)
    specs = [pl.BlockSpec(memory_space=pltpu.SMEM)] + [vmem] * 5
    out = jax.ShapeDtypeStruct((2, 4) + piece, BF16)
    return call(functools.partial(self_kernel, width), ident, out, scratch, operands, specs)


def cross_kernel(width, length_ref, after_ref, gain_ref, weight_ref, both_ref, out_ref, result_ref, *refs):
    blocks, got_y, ctx, got_ctx, terms, y_s, y_r, c_s, c_r, got_zh, zh_s, zh_r, relay = refs[:13]
    near = refs[13:]
    half = near[3]
    y, zh = place_on(LINE_Y), place_on(LINE_ZH)
    v = lax.axis_index("vocab")
    side = peers_on(LINE_Y)
    devices = peers_on(LINE_CORE) + peers_on(LINE_X) + peers_on(LINE_ZH) + side
    barrier = greet(devices)
    row = after_ref.shape[0] // 2
    own = row // 4
    cols = 2 * DH
    gain = quarter_of(gain_ref)
    weight = weight_ref[:, 3].reshape(after_ref.shape[1], 2 * DH)
    share = pl.ds(pl.multiple_of((v // 2) * cols, cols), cols)
    for pair in range(2):
        wide = after_ref[pair * row : (pair + 1) * row].astype(F32)
        squares = jnp.sum(wide * wide, axis=-1, keepdims=True)
        scaled = (wide * gain).astype(BF16)
        product = jnp.dot(scaled, weight, preferred_element_type=F32)
        for head in range(2):
            queries = pltpu.roll(product, DH, 1) if head else product
            blocks[2 * pair + head, :row] = with_squares(queries, squares, DH).astype(BF16)
        for k in range(4):
            lower = pair * row + k * own
            blocks[k, row + pair * own : row + (pair + 1) * own] = after_ref[lower : lower + own, share]
    pl.semaphore_wait(barrier, len(devices))
    exchange_y(blocks, got_y, relay, y_s, y_r)
    query = scaled_sum(got_y, row, DH, width)
    query = jnp.where(lanes_of(query.shape) < DH, query, 0.0).astype(BF16)
    both = both_ref[...]
    visible = lanes_of((row, both.shape[0])) < length_ref[y // 2]
    ctx[...] = attend(query, both, visible, lax.rem(y, 2)).reshape(ctx.shape)
    copies = []
    for k in range(3):
        other = lax.rem(y + k + 1, 4)
        copies.append(send(ctx.at[other], got_ctx.at[y], side[k], c_s.at[k], c_r.at[k]))
    got_ctx[y] = ctx[y]
    for copy in copies:
        copy.wait()
    context = jnp.concatenate([got_ctx[0] + got_ctx[1], got_ctx[2] + got_ctx[3]], axis=0)
    out_cols = terms.shape[4]
    for core in range(2):
        for place in range(4):
            for far in range(2):
                lower = (far * 8 + place * 2 + core) * out_cols
                product = jnp.dot(context, out_ref[:, lower : lower + out_cols], preferred_element_type=F32)
                terms[core, place, far] = product.astype(BF16)
    near_sum(terms, *near)
    send(half.at[1 - zh], got_zh, peers_on(LINE_ZH)[0], zh_s.at[0], zh_r.at[0]).wait()
    total = half[zh].astype(F32) + got_zh[...].astype(F32)
    first = 2 * lax.rem(v, 2)
    for k in range(2):
        residual = got_y[first + k, row:].astype(F32)
        lanes = slice(k * cols, (k + 1) * cols)
        result_ref[:, lanes] = (residual + total[:, lanes]).astype(BF16)


def cross_block(ident, width, length, after, gain, weights, both, out_weight):
    row = after.shape[0] // 2
    own = row // 4
    block = (2, 2 * own, width // 16)
    vmem = pl.BlockSpec(memory_space=pltpu.VMEM)
    scratch = (
        [
            pltpu.VMEM((4, row + 2 * own, 2 * DH), BF16),
            pltpu.VMEM((4, row + 2 * own, 2 * DH), BF16),
            pltpu.VMEM((4, own, 2 * DH), BF16),
            pltpu.VMEM((4, own, 2 * DH), BF16),
            pltpu.VMEM((2, 4) + block, BF16),
        ]
        + sems(6) + sems(3) + [pltpu.VMEM(block[1:], BF16)] + sems(1)
        + [half_pair((row + 2 * own, 2 * DH))] + near_sum_scratch(block)
    )
    operands = (length, after, gain, weights, both, out_weight)
    specs = [pl.BlockSpec(memory_space=pltpu.SMEM)] + [vmem] * 5
    out = jax.ShapeDtypeStruct(block[1:], BF16)
    return call(functools.partial(cross_kernel, width), ident, out, scratch, operands, specs)


def on_device(
    token_ids,
    keep_mask,
    target_length,
    source_length,
    embed_table,
    self_gain,
    query_weight,
    key_weight,
    value_weight,
    self_out_weight,
    cross_gain,
    cross_query_weight,
    cross_keys,
    cross_values,
    cross_out_weight,
):
    pairs, tokens = token_ids.shape
    vocab_index = lax.axis_index("vocab")
    n_y, n_z = LINE_Y[1], LINE_Z[1]
    width = self_gain.shape[0]
    quarter = width // n_y
    cols = embed_table.shape[1]
    row_tokens = pairs * n_y * tokens
    pieces = 8
    piece = row_tokens // pieces

    same_y = [[z * n_y + y for z in range(n_z)] for y in range(n_y)]
    weights = jnp.stack([key_weight, value_weight, query_weight, cross_query_weight])
    weights = lax.all_gather(weights, "seq", axis_index_groups=same_y)

    ids = jnp.where(keep_mask != 0, token_ids, -1).reshape(1, pairs * tokens)
    both_shape = (n_y, cross_keys.shape[1], 2 * DH)
    out = (
        jax.ShapeDtypeStruct((n_z, n_y) + ids.shape, ids.dtype),
        jax.ShapeDtypeStruct(both_shape, BF16),
    )
    scratch = [
        pltpu.VMEM((n_y,) + ids.shape, ids.dtype),
        pltpu.VMEM(both_shape, BF16),
        pltpu.SemaphoreType.DMA((2,)),
    ]
    operands = (ids, cross_keys, cross_values)
    ids, both = call(start_kernel, 0, out, scratch + sems(3) + sems(7) + sems(3), operands)
    ids = ids.reshape(n_z, n_y, pairs, tokens).transpose(0, 2, 1, 3)
    ids = ids.reshape(n_z, pieces, piece).transpose(1, 0, 2).reshape(-1)

    shard_rows = embed_table.shape[0]
    local_ids = ids - vocab_index * shard_rows
    inside = (local_ids >= 0) & (local_ids < shard_rows)
    picked = jnp.take(embed_table, jnp.clip(local_ids, 0, shard_rows - 1), axis=0)
    picked = jnp.where(inside[:, None], picked, jnp.zeros_like(picked))
    own_rows, embedded, both = embed_rows(picked.reshape(2, 4, n_z, piece, cols), both, 1)
    both = both.reshape(-1, 2 * DH)
    embedded = embedded.reshape(row_tokens, quarter)

    gains = [gain.reshape(1, width) for gain in (self_gain, cross_gain)]
    after = self_block(2, width, target_length, embedded, own_rows, gains[0], weights, self_out_weight)
    after = after.reshape(row_tokens, quarter)
    result = cross_block(3, width, source_length, after, gains[1], weights, both, cross_out_weight)
    return result.reshape(pairs, tokens, result.shape[1])


def solution(mesh):
    return jax.shard_map(
        on_device,
        mesh=mesh,
        in_specs=(
            P(None, "seq"),
            P(None, "seq"),
            P(),
            P(),
            P("vocab", "seq"),
            P(),
            P("seq", "vocab"),
            P("seq", "vocab"),
            P("seq", "vocab"),
            P("vocab", None),
            P(),
            P("seq", "vocab"),
            P(None, "seq", "vocab"),
            P(None, "seq", "vocab"),
            P("vocab", None),
        ),
        out_specs=P(None, "seq", "vocab"),
        check_vma=False,
    )
```

```python
import functools

import jax
import jax.numpy as jnp
from jax import lax
from jax.experimental import pallas as pl
from jax.experimental.pallas import tpu as pltpu
from jax.sharding import PartitionSpec as P

DH = 64
MESH = pl.DeviceIdType.MESH
F32 = jnp.float32
BF16 = jnp.bfloat16

LINE_Y = ("seq", 4, 1)
LINE_Z = ("seq", 8, 4)
LINE_CORE = ("vocab", 2, 1)
LINE_X = ("vocab", 4, 2)
LINE_ZH = ("vocab", 2, 8)


def place_on(line):
    axis, members, stride = line
    return lax.rem(lax.axis_index(axis) // stride, members)


def peer_of(line, shift):
    axis, members, stride = line
    here = lax.axis_index(axis)
    mine = lax.rem(here // stride, members)
    other = lax.rem(mine + shift, members)
    there = here + (other - mine) * stride
    if axis == "seq":
        return (lax.axis_index("vocab"), there), other
    return (there, lax.axis_index("seq")), other


def greet(devices):
    barrier = pltpu.get_barrier_semaphore()
    for target in devices:
        pl.semaphore_signal(barrier, inc=1, device_id=target, device_id_type=MESH)
    return barrier


def peers_on(line):
    return [peer_of(line, shift)[0] for shift in range(1, line[1])]


def send(source, target_ref, target, send_sem, recv_sem):
    copy = pltpu.make_async_remote_copy(
        src_ref=source,
        dst_ref=target_ref,
        send_sem=send_sem,
        recv_sem=recv_sem,
        device_id=target,
        device_id_type=MESH,
    )
    copy.start()
    return copy


def lanes_of(shape):
    return lax.broadcasted_iota(jnp.int32, shape, 1)


def by_head(left, right):
    low = lanes_of(left.shape) < DH
    return jnp.where(low, left, pltpu.roll(right, DH, 1)), jnp.where(low, pltpu.roll(left, DH, 1), right)


def quarter_of(ref):
    cols = ref.shape[1] // 32
    starts = [pl.multiple_of((4 * k + place_on(LINE_Y)) * cols, cols) for k in range(8)]
    return jnp.concatenate([ref[:, pl.ds(start, cols)] for start in starts], axis=1)


def start_kernel(ids_ref, keys_ref, values_ref, all_ids, both_out, row_ids, both_ref, own, y_s, y_r, z_s, z_r, b_s, b_r):
    y, z = place_on(LINE_Y), place_on(LINE_Z)
    near, far = peers_on(LINE_Y), peers_on(LINE_Z)
    barrier = greet(near + far)
    keep = pltpu.make_async_copy(ids_ref, row_ids.at[y], own.at[0])
    keep.start()
    for pair in range(2):
        first, second = by_head(keys_ref[pair].astype(F32), values_ref[pair].astype(F32))
        both_ref[2 * pair] = first.astype(BF16)
        both_ref[2 * pair + 1] = second.astype(BF16)
    both_out[y] = both_ref[y]
    pl.semaphore_wait(barrier, len(near + far))
    copies = [send(ids_ref, row_ids.at[y], near[k], y_s.at[k], y_r.at[k]) for k in range(3)]
    later = []
    for k in range(3):
        other = lax.rem(y + k + 1, 4)
        later.append(send(both_ref.at[other], both_out.at[y], near[k], b_s.at[k], b_r.at[k]))
    for copy in [keep] + copies:
        copy.wait()
    last = pltpu.make_async_copy(row_ids, all_ids.at[z], own.at[1])
    last.start()
    later += [send(row_ids, all_ids.at[z], far[k], z_s.at[k], z_r.at[k]) for k in range(7)]
    for copy in later + [last]:
        copy.wait()


def sems(count):
    return [pltpu.SemaphoreType.DMA((count,))] * 2


def call(kernel, ident, out, scratch, operands, in_specs=None):
    vmem = pl.BlockSpec(memory_space=pltpu.VMEM)
    return pl.pallas_call(
        kernel,
        out_shape=out,
        in_specs=in_specs or [vmem] * len(operands),
        out_specs=(vmem,) * len(out) if isinstance(out, tuple) else vmem,
        scratch_shapes=scratch,
        compiler_params=pltpu.CompilerParams(collective_id=ident, has_side_effects=True),
    )(*operands)


def chunks_of(ref):
    middle = ref.shape[0] // 2
    return [slice(0, middle), slice(middle, 2 * middle)]


def near_sum(x_ref, got_core, part, got_x, half, core_s, core_r, x_s, x_r, then=None):
    core, place = place_on(LINE_CORE), place_on(LINE_X)
    twin, row = peers_on(LINE_CORE)[0], peers_on(LINE_X)
    order = (1, 2, 3, 0)
    chunks = chunks_of(half)
    core_copies = []
    for c, rows in enumerate(chunks):
        for k, shift in enumerate(order):
            other = lax.rem(place + shift, 4)
            source, landing = x_ref.at[1 - core, other, rows], got_core.at[other, rows]
            core_copies.append(send(source, landing, twin, core_s.at[4 * c + k], core_r.at[4 * c + k]))
    x_copies = []
    for c, rows in enumerate(chunks):
        for k, shift in enumerate(order):
            other = lax.rem(place + shift, 4)
            core_copies[4 * c + k].wait()
            term = x_ref[core, other, rows].astype(F32) + got_core[other, rows].astype(F32)
            part[other, rows] = term.astype(BF16)
            if shift:
                index = 3 * c + k
                landing = got_x.at[k, rows]
                x_copies.append(send(part.at[other, rows], landing, row[k], x_s.at[index], x_r.at[index]))
    for c, rows in enumerate(chunks):
        total = part[place, rows].astype(F32)
        for k in range(3):
            x_copies[3 * c + k].wait()
            total = total + got_x[k, rows].astype(F32)
        half[rows] = total.astype(BF16)
        if then is not None:
            then(c, rows)


def near_sum_scratch(block):
    return [
        pltpu.VMEM((4,) + block, BF16),
        pltpu.VMEM((4,) + block, BF16),
        pltpu.VMEM((3,) + block, BF16),
        pltpu.VMEM(block, BF16),
    ] + sems(8) + sems(6)


def spread(block, all_ref, core_s, core_r, x_s, x_r, local, fill=None):
    core, place = place_on(LINE_CORE), place_on(LINE_X)
    twin, row = peers_on(LINE_CORE)[0], peers_on(LINE_X)
    chunks = chunks_of(block)
    copies, x_copies = [], []
    for c, rows in enumerate(chunks):
        if fill is not None:
            fill(c, rows)
        landing = all_ref.at[core, place, rows]
        for k in range(3):
            index = 3 * c + k
            x_copies.append(send(block.at[rows], landing, row[k], x_s.at[index], x_r.at[index]))
        copies.append(send(block.at[rows], landing, twin, core_s.at[4 * c], core_r.at[4 * c]))
    keep = pltpu.make_async_copy(block, all_ref.at[core, place], local)
    keep.start()
    for c, rows in enumerate(chunks):
        for k in range(3):
            x_copies[3 * c + k].wait()
            source = all_ref.at[core, lax.rem(place + 3 - k, 4), rows]
            index = 4 * c + k + 1
            copies.append(send(source, source, twin, core_s.at[index], core_r.at[index]))
    for copy in copies:
        copy.wait()
    keep.wait()


def spread_scratch():
    return sems(8) + sems(6) + [pltpu.SemaphoreType.DMA]


def rows_kernel(x_ref, both_ref, own_ref, all_ref, all_both, *refs):
    near, refs = refs[:8], refs[8:]
    got, z_s, z_r, zh_s, zh_r, b_s, b_r = refs[:7]
    half = near[3]
    z, zh = place_on(LINE_Z), place_on(LINE_ZH)
    v, s = lax.axis_index("vocab"), lax.axis_index("seq")
    level = peers_on(LINE_Z)
    over_v = peer_of(LINE_ZH, 1)[0][0]
    across = [(over_v, peer_of(LINE_Z, k)[0][1]) for k in range(8)]
    devices = peers_on(LINE_CORE) + peers_on(LINE_X) + level + across
    barrier = greet(devices)
    pl.semaphore_wait(barrier, len(devices))
    late = [send(both_ref, all_both.at[z], level[k], b_s.at[k], b_r.at[k]) for k in range(7)]
    all_both[z] = both_ref[...]
    near_sum(x_ref, *near)
    copies = []
    for k in (4, 3, 5, 2, 6, 1, 7, 0):
        other = lax.rem(z + k, 8)
        copies.append(send(half.at[other], got.at[zh, z], across[k], zh_s.at[k], zh_r.at[k]))
        if k:
            copies.append(send(half.at[other], got.at[zh, z], level[k - 1], z_s.at[k - 1], z_r.at[k - 1]))
    got[zh, z] = half[z]
    for copy in copies:
        copy.wait()
    cols = got.shape[3]
    for k in range(8):
        own_ref[:, k * cols : (k + 1) * cols] = (got[0, k].astype(F32) + got[1, k].astype(F32)).astype(BF16)
    spread(own_ref, all_ref, *refs[7:])
    for copy in late:
        copy.wait()


def embed_rows(x, both, ident):
    block = x.shape[2:]
    own = (block[1], block[0] * block[2])
    out = tuple(jax.ShapeDtypeStruct(shape, BF16) for shape in (own, (2, 4) + own, (8,) + both.shape))
    scratch = near_sum_scratch(block) + [pltpu.VMEM((2,) + block, BF16)]
    scratch += sems(7) + sems(8) + sems(7) + spread_scratch()
    return call(rows_kernel, ident, out, scratch, (x, both))


def with_squares(product, squares, lane):
    high = squares.astype(BF16).astype(F32)
    at = lanes_of(product.shape)
    return jnp.where(at == lane, high, jnp.where(at == lane + 1, squares - high, product))


def scaled_sum(got, rows, lane, width):
    total = got[0, :rows].astype(F32)
    for k in range(1, 4):
        total = total + got[k, :rows].astype(F32)
    squares = total[:, lane : lane + 1] + total[:, lane + 1 : lane + 2]
    return total * lax.rsqrt(squares / width + 1e-06)


def attend(query, both, visible, head):
    scores = lax.dot_general(query, both, (((1,), (1,)), ((), ())), preferred_element_type=F32)
    scores = jnp.where(visible, scores, -jnp.inf)
    raised = jnp.exp(scores - jnp.max(scores, axis=-1, keepdims=True))
    totals = jnp.sum(raised, axis=-1, keepdims=True)
    mixed = jnp.dot(raised.astype(BF16), both, preferred_element_type=F32) / totals
    moved = jnp.where(head == 0, pltpu.roll(mixed, DH, 1), mixed)
    return jnp.where(lanes_of(moved.shape) // DH == head, moved, 0.0).astype(BF16)


def self_kernel(width, length_ref, emb_ref, own_ref, gain_ref, weight_ref, out_ref, all_ref, *refs):
    blocks, got_y, kv, got_ctx, terms, y_s, y_r, up_s, up_r, c_s, c_r, got_zh, piece, zh_s, zh_r = refs[:15]
    near, far = refs[15:23], refs[23:]
    half = near[3]
    y, z = place_on(LINE_Y), place_on(LINE_Z)
    side = peers_on(LINE_Y)
    up, down = peer_of(LINE_Z, 1)[0], peer_of(LINE_Z, 7)[0]
    has_up, has_down = z < 7, z > 0
    devices = peers_on(LINE_CORE) + peers_on(LINE_X) + peers_on(LINE_ZH) + side
    barrier = greet(devices)

    @pl.when(has_up)
    def _():
        pl.semaphore_signal(barrier, inc=1, device_id=up, device_id_type=MESH)

    @pl.when(has_down)
    def _():
        pl.semaphore_signal(barrier, inc=1, device_id=down, device_id_type=MESH)

    row, quarter = emb_ref.shape[0] // 2, emb_ref.shape[1]
    gain = quarter_of(gain_ref)
    weights = [weight_ref[:, k].reshape(quarter, 2 * DH) for k in range(3)]
    for pair in range(2):
        wide = emb_ref[pair * row : (pair + 1) * row].astype(F32)
        squares = jnp.sum(wide * wide, axis=-1, keepdims=True)
        scaled = (wide * gain).astype(BF16)
        keys, values, queries = (jnp.dot(scaled, weight, preferred_element_type=F32) for weight in weights)
        kv_heads = by_head(keys, values)
        q_heads = (queries, pltpu.roll(queries, DH, 1))
        for head in range(2):
            blocks[2 * pair + head, :, : 2 * DH] = kv_heads[head].astype(BF16)
            blocks[2 * pair + head, :, 2 * DH :] = with_squares(q_heads[head], squares, DH).astype(BF16)
    for k in range(1, 8):

        @pl.when(k > z)
        def _():
            kv[k] = jnp.zeros(kv.shape[1:], BF16)

    @pl.when(has_up & has_down)
    def _():
        pl.semaphore_wait(barrier, len(devices) + 2)

    @pl.when(jnp.logical_not(has_up & has_down))
    def _():
        pl.semaphore_wait(barrier, len(devices) + 1)

    copies = []
    for k in range(3):
        other = lax.rem(y + k + 1, 4)
        copies.append(send(blocks.at[other], got_y.at[y], side[k], y_s.at[k], y_r.at[k]))
    got_y[y] = blocks[y]
    for copy in copies:
        copy.wait()
    qkv = scaled_sum(got_y, row, 3 * DH, width)
    kv[z] = qkv[:, : 2 * DH].astype(BF16)
    query = qkv[:, 2 * DH :]
    query = jnp.where(lanes_of(query.shape) < DH, query, 0.0).astype(BF16)

    chunk = row // 2

    def passing(source, step, part):
        place = kv.at[source, part * chunk : (part + 1) * chunk]
        index = (step - 1) * 2 + part
        return pltpu.make_async_remote_copy(
            src_ref=place,
            dst_ref=place,
            send_sem=up_s.at[index],
            recv_sem=up_r.at[index],
            device_id=up,
            device_id_type=MESH,
        )

    for step in range(1, 9):
        for part in range(2):
            if step > 1:

                @pl.when(z - step + 1 >= 0)
                def _():
                    passing(z - step + 1, step - 1, part).wait_recv()

            if step < 8:

                @pl.when(has_up & (z - step + 1 >= 0))
                def _():
                    passing(z - step + 1, step, part).start()

    pair = y // 2
    both = kv[...].reshape(8 * row, 2 * DH)
    key_pos = lanes_of((row, 8 * row))
    query_pos = z * row + lax.broadcasted_iota(jnp.int32, (row, 8 * row), 0)
    visible = (key_pos <= query_pos) & (key_pos < length_ref[pair])
    got_ctx[y] = attend(query, both, visible, lax.rem(y, 2))
    copies = [send(got_ctx.at[y], got_ctx.at[y], side[k], c_s.at[k], c_r.at[k]) for k in range(3)]
    for step in range(1, 8):
        for part in range(2):

            @pl.when(has_up & (z - step + 1 >= 0))
            def _():
                passing(z - step + 1, step, part).wait_send()

    for copy in copies:
        copy.wait()
    out_part = quarter_of(out_ref)
    for pair in range(2):
        context = got_ctx[2 * pair] + got_ctx[2 * pair + 1]
        product = jnp.dot(context, out_part, preferred_element_type=F32).astype(BF16)
        terms[pair] = product.reshape(terms.shape[1:])
    crossing = []

    def cross_over(c, rows):
        target = peers_on(LINE_ZH)[0]
        crossing.append(send(half.at[rows], got_zh.at[rows], target, zh_s.at[c], zh_r.at[c]))

    def fill(c, rows):
        crossing[c].wait()
        total = half[rows].astype(F32) + got_zh[rows].astype(F32)
        piece[rows] = (own_ref[rows].astype(F32) + total).astype(BF16)

    near_sum(terms, *near, then=cross_over)
    spread(piece, all_ref, *far, fill=fill)


def self_block(ident, width, length, embedded, own_rows, gain, weights, out_weight):
    tokens, quarter = embedded.shape
    row = tokens // 2
    piece = own_rows.shape
    vmem = pl.BlockSpec(memory_space=pltpu.VMEM)
    scratch = (
        [
            pltpu.VMEM((4, row, 4 * DH), BF16),
            pltpu.VMEM((4, row, 4 * DH), BF16),
            pltpu.VMEM((8, row, 2 * DH), BF16),
            pltpu.VMEM((4, row, 2 * DH), BF16),
            pltpu.VMEM((2, 4) + piece, BF16),
        ]
        + sems(3) + sems(14) + sems(3)
        + [pltpu.VMEM(piece, BF16), pltpu.VMEM(piece, BF16)]
        + sems(2) + near_sum_scratch(piece) + spread_scratch()
    )
    operands = (length, embedded, own_rows, gain, weights, out_weight)
    specs = [pl.BlockSpec(memory_space=pltpu.SMEM)] + [vmem] * 5
    out = jax.ShapeDtypeStruct((2, 4) + piece, BF16)
    return call(functools.partial(self_kernel, width), ident, out, scratch, operands, specs)


def cross_kernel(width, length_ref, after_ref, gain_ref, weight_ref, both_ref, out_ref, result_ref, *refs):
    blocks, got_y, ctx, got_ctx, terms, y_s, y_r, c_s, c_r, got_zh, zh_s, zh_r = refs[:12]
    near = refs[12:]
    half = near[3]
    y, zh = place_on(LINE_Y), place_on(LINE_ZH)
    v = lax.axis_index("vocab")
    side = peers_on(LINE_Y)
    devices = peers_on(LINE_CORE) + peers_on(LINE_X) + peers_on(LINE_ZH) + side
    barrier = greet(devices)
    row = after_ref.shape[0] // 2
    own = row // 4
    cols = 2 * DH
    gain = quarter_of(gain_ref)
    weight = weight_ref[:, 3].reshape(after_ref.shape[1], 2 * DH)
    share = pl.ds(pl.multiple_of((v // 2) * cols, cols), cols)
    for pair in range(2):
        wide = after_ref[pair * row : (pair + 1) * row].astype(F32)
        squares = jnp.sum(wide * wide, axis=-1, keepdims=True)
        scaled = (wide * gain).astype(BF16)
        product = jnp.dot(scaled, weight, preferred_element_type=F32)
        for head in range(2):
            queries = pltpu.roll(product, DH, 1) if head else product
            blocks[2 * pair + head, :row] = with_squares(queries, squares, DH).astype(BF16)
        for k in range(4):
            lower = pair * row + k * own
            blocks[k, row + pair * own : row + (pair + 1) * own] = after_ref[lower : lower + own, share]
    pl.semaphore_wait(barrier, len(devices))
    copies = []
    for k in range(3):
        other = lax.rem(y + k + 1, 4)
        copies.append(send(blocks.at[other], got_y.at[y], side[k], y_s.at[k], y_r.at[k]))
    got_y[y] = blocks[y]
    for copy in copies:
        copy.wait()
    query = scaled_sum(got_y, row, DH, width)
    query = jnp.where(lanes_of(query.shape) < DH, query, 0.0).astype(BF16)
    both = both_ref[...]
    visible = lanes_of((row, both.shape[0])) < length_ref[y // 2]
    ctx[...] = attend(query, both, visible, lax.rem(y, 2)).reshape(ctx.shape)
    copies = []
    for k in range(3):
        other = lax.rem(y + k + 1, 4)
        copies.append(send(ctx.at[other], got_ctx.at[y], side[k], c_s.at[k], c_r.at[k]))
    got_ctx[y] = ctx[y]
    for copy in copies:
        copy.wait()
    context = jnp.concatenate([got_ctx[0] + got_ctx[1], got_ctx[2] + got_ctx[3]], axis=0)
    out_cols = terms.shape[4]
    for core in range(2):
        for place in range(4):
            for far in range(2):
                lower = (far * 8 + place * 2 + core) * out_cols
                product = jnp.dot(context, out_ref[:, lower : lower + out_cols], preferred_element_type=F32)
                terms[core, place, far] = product.astype(BF16)
    near_sum(terms, *near)
    send(half.at[1 - zh], got_zh, peers_on(LINE_ZH)[0], zh_s.at[0], zh_r.at[0]).wait()
    total = half[zh].astype(F32) + got_zh[...].astype(F32)
    first = 2 * lax.rem(v, 2)
    for k in range(2):
        residual = got_y[first + k, row:].astype(F32)
        lanes = slice(k * cols, (k + 1) * cols)
        result_ref[:, lanes] = (residual + total[:, lanes]).astype(BF16)


def cross_block(ident, width, length, after, gain, weights, both, out_weight):
    row = after.shape[0] // 2
    own = row // 4
    block = (2, 2 * own, width // 16)
    vmem = pl.BlockSpec(memory_space=pltpu.VMEM)
    scratch = (
        [
            pltpu.VMEM((4, row + 2 * own, 2 * DH), BF16),
            pltpu.VMEM((4, row + 2 * own, 2 * DH), BF16),
            pltpu.VMEM((4, own, 2 * DH), BF16),
            pltpu.VMEM((4, own, 2 * DH), BF16),
            pltpu.VMEM((2, 4) + block, BF16),
        ]
        + sems(3) + sems(3) + [pltpu.VMEM(block[1:], BF16)] + sems(1) + near_sum_scratch(block)
    )
    operands = (length, after, gain, weights, both, out_weight)
    specs = [pl.BlockSpec(memory_space=pltpu.SMEM)] + [vmem] * 5
    out = jax.ShapeDtypeStruct(block[1:], BF16)
    return call(functools.partial(cross_kernel, width), ident, out, scratch, operands, specs)


def on_device(
    token_ids,
    keep_mask,
    target_length,
    source_length,
    embed_table,
    self_gain,
    query_weight,
    key_weight,
    value_weight,
    self_out_weight,
    cross_gain,
    cross_query_weight,
    cross_keys,
    cross_values,
    cross_out_weight,
):
    pairs, tokens = token_ids.shape
    vocab_index = lax.axis_index("vocab")
    n_y, n_z = LINE_Y[1], LINE_Z[1]
    width = self_gain.shape[0]
    quarter = width // n_y
    cols = embed_table.shape[1]
    row_tokens = pairs * n_y * tokens
    pieces = 8
    piece = row_tokens // pieces

    same_y = [[z * n_y + y for z in range(n_z)] for y in range(n_y)]
    weights = jnp.stack([key_weight, value_weight, query_weight, cross_query_weight])
    weights = lax.all_gather(weights, "seq", axis_index_groups=same_y)

    ids = jnp.where(keep_mask != 0, token_ids, -1).reshape(1, pairs * tokens)
    both_shape = (n_y, cross_keys.shape[1], 2 * DH)
    out = (
        jax.ShapeDtypeStruct((n_z, n_y) + ids.shape, ids.dtype),
        jax.ShapeDtypeStruct(both_shape, BF16),
    )
    scratch = [
        pltpu.VMEM((n_y,) + ids.shape, ids.dtype),
        pltpu.VMEM(both_shape, BF16),
        pltpu.SemaphoreType.DMA((2,)),
    ]
    operands = (ids, cross_keys, cross_values)
    ids, both = call(start_kernel, 0, out, scratch + sems(3) + sems(7) + sems(3), operands)
    ids = ids.reshape(n_z, n_y, pairs, tokens).transpose(0, 2, 1, 3)
    ids = ids.reshape(n_z, pieces, piece).transpose(1, 0, 2).reshape(-1)

    shard_rows = embed_table.shape[0]
    local_ids = ids - vocab_index * shard_rows
    inside = (local_ids >= 0) & (local_ids < shard_rows)
    picked = jnp.take(embed_table, jnp.clip(local_ids, 0, shard_rows - 1), axis=0)
    picked = jnp.where(inside[:, None], picked, jnp.zeros_like(picked))
    own_rows, embedded, both = embed_rows(picked.reshape(2, 4, n_z, piece, cols), both, 1)
    both = both.reshape(-1, 2 * DH)
    embedded = embedded.reshape(row_tokens, quarter)

    gains = [gain.reshape(1, width) for gain in (self_gain, cross_gain)]
    after = self_block(2, width, target_length, embedded, own_rows, gains[0], weights, self_out_weight)
    after = after.reshape(row_tokens, quarter)
    result = cross_block(3, width, source_length, after, gains[1], weights, both, cross_out_weight)
    return result.reshape(pairs, tokens, result.shape[1])


def solution(mesh):
    return jax.shard_map(
        on_device,
        mesh=mesh,
        in_specs=(
            P(None, "seq"),
            P(None, "seq"),
            P(),
            P(),
            P("vocab", "seq"),
            P(),
            P("seq", "vocab"),
            P("seq", "vocab"),
            P("seq", "vocab"),
            P("vocab", None),
            P(),
            P("seq", "vocab"),
            P(None, "seq", "vocab"),
            P(None, "seq", "vocab"),
            P("vocab", None),
        ),
        out_specs=P(None, "seq", "vocab"),
        check_vma=False,
    )
```
